32 devices in a mesh: lat: 8 (over y, x, core), lon: 4 (over z).
Axes of the slice: x: 2, y: 2, z: 4, core: 2. Of those that a mesh axis runs over, the one named last changes fastest.
Arguments:
- adjoint_in: float32 [2, 24, 128, 2880], P(None, None, 'lat', 'lon'), may hold values from -6 to 6
- wind_east: float32 [24, 128, 2880], P(None, 'lat', 'lon'), may hold values from -0.45 to 0.45
- wind_north: float32 [24, 128, 2880], P(None, 'lat', 'lon'), may hold values from -0.45 to 0.45
- polar_mask: int32 [128], replicated, may hold values from 0 to 1, as said below
- obs_owner: int32 [131072, 1], P(('lat', 'lon')), may hold values from 0 to 31; in each aligned block of 4096 rows (0 to 4095, 4096 to 8191, ...) at most 256 rows name the same one
- obs_cell: int32 [131072], P(('lat', 'lon')), may hold values from 0 to 11519
- obs_kernel: float32 [131072, 24], P(('lat', 'lon')), may hold values from 0.2 to 2
- obs_resid: float32 [131072, 2], P(('lat', 'lon')), may hold values from -6 to 6
Outputs:
- adjoint_out: float32 [2, 24, 128, 2880], P(None, None, 'lat', 'lon')
The draws below stay inside these ranges and needn't reach their ends.
Inputs may be any that keep to these rules, and one draw needn't show every extreme that they name: polar_mask is 1 exactly on the first KS rows and the last KN rows, with KS and KN each from 1 to 16 and one of them equal to 16. `obs_owner`: among the soundings of one device no owner is named more than 256 times, and in every draw some device names some owner exactly 256 times.
All inputs are finite; a program needn't handle non-finite values.
Results may differ from the reference program's by a relative error of at most 0.00008.
Values sent between devices are 32-bit elements; how exact they have to be, the bound alone decides.
A program may use at most 128 MiB of HBM per device.

```python
import math
import jax
import jax.numpy as jnp
import numpy as np

NLON = 2880
TRACERS = 2
LEV = 24
LAT_DEV = 16
OBS_DEV = 4096
LON_DEV = 720
NLAT = 128
POLAR_MAX = 16
CAP = 256
NOBS = 131072
N_LON = 4
DEVICES = 32


def draw_polar_mask(key, part):
    key_side = jax.random.fold_in(key, 11)
    key_count = jax.random.fold_in(key, 23)
    other_count = jax.random.randint(key_count, (), 1, POLAR_MAX + 1)
    flipped = jax.random.randint(key_side, (), 0, 2)
    north_count = jnp.where(flipped == 1, POLAR_MAX, other_count)
    south_count = jnp.where(flipped == 1, other_count, POLAR_MAX)
    row_ids = jnp.arange(NLAT)
    return ((row_ids < south_count) | (row_ids >= NLAT - north_count)).astype(jnp.int32)


def set_ends(array, stream_key, smallest, high):
    extent = array.shape
    index_at = [jax.random.randint(jax.random.fold_in(stream_key, axis), (), 0, extent[axis]) for axis in range(len(extent))]
    array = array.at[tuple(index_at)].set(smallest)
    longest = extent.index(max(extent))
    index_at[longest] = (index_at[longest] + 1) % extent[longest]
    return array.at[tuple(index_at)].set(high)


def block_scale(stream_key, extent, shards, least, top_value):
    gain, own = 1.0, jax.random.fold_in(stream_key, 6)
    for dim, blocks in shards:
        heights = jnp.exp(jax.random.uniform(jax.random.fold_in(own, dim), (blocks,), jnp.float32, least / len(shards), top_value / len(shards)))
        gain = gain * jnp.repeat(heights, extent[dim] // blocks).reshape([-1 if axis == dim else 1 for axis in range(len(extent))])
    return gain


def routed_block(own_key, own, number, rows, number_of, top, most, lean):
    sequence = jax.random.permutation(own_key, number_of)
    crowded, usual = portions_of(number_of, rows * top, most, lean, True), portions_of(number_of, rows * top, most, lean, False)
    places = jnp.arange(number_of)

    def named(sizes, rotation):
        used = int((sizes > 0).sum())
        fixed = max(1, used // 4)
        moved = fixed + (places - fixed + rotation * (used - fixed)) % max(1, number_of - fixed)
        return jnp.zeros((number_of,), jnp.int32).at[sequence[jnp.where(places < fixed, places, moved)]].set(jnp.asarray(sizes, jnp.int32))

    sizes = jnp.where(number % 4 == 0, named(crowded, number // 4), named(usual, number - number // 4 - 1))
    mixed = jax.random.permutation(jax.random.fold_in(own, 3), number_of)
    donor, sink = mixed[0:number_of // 2 * 2:2], mixed[1:number_of // 2 * 2:2]
    margin = jnp.minimum(sizes[donor] - 1, most - sizes[sink]) // 2
    margin = jnp.where((donor == sequence[0]) | (sink == sequence[0]) | (sizes[sink] == 0), 0, jnp.maximum(margin, 0))
    moved = jax.random.randint(jax.random.fold_in(own, 4), (number_of // 2,), 0, 1 << 20) % (margin + 1)
    sizes = sizes.at[donor].add(-moved).at[sink].add(moved)
    members = jnp.searchsorted(jnp.cumsum(sizes), jnp.arange(rows * top), side="right").astype(jnp.int32)
    listing = members.reshape(top, rows).T
    listing = listing[jax.random.permutation(jax.random.fold_in(own, 1), rows)]
    rotation = jax.random.randint(jax.random.fold_in(own, 2), (rows, 1), 0, top)
    return jnp.take_along_axis(listing, (jnp.arange(top)[None, :] + rotation) % top, axis=1)


def portions_of(amount, total, reach, lean, full):
    portions = [(1 << 20) // math.isqrt(rank ** lean) + 1 for rank in range(1, amount + 1)]
    largest = reach if full else min(reach, max(-(-total // amount), total * portions[0] // sum(portions)))
    least = 1 if total - largest >= amount - 1 else 0
    counts, spare = [largest] + [least] * (amount - 1), total - largest - least * (amount - 1)
    while spare > 0:
        candidates = [i for i in range(1, amount) if counts[i] < largest] or [i for i in range(1, amount) if counts[i] < reach]
        pool, left = sum([portions[i] for i in candidates]), spare
        for i in candidates:
            extra = min(reach - counts[i], max(1, left * portions[i] // pool), spare)
            counts[i] = counts[i] + extra
            spare = spare - extra
    return np.array(counts)


def noise(stream_key, dims, deviation, bound, pieces=(), held_as=jnp.bfloat16):
    entries = jax.random.normal(stream_key, dims, jnp.float32) * deviation
    if len(pieces) > 0:
        entries = block_scale(stream_key, dims, pieces, -0.22, 0.18) * entries
    return jnp.clip(entries, min=-bound, max=bound).astype(held_as)


def setup_inputs(seed: int = 0) -> dict:
    key_list = jax.random.split(jax.random.key(seed), 9)
    adjoint_in = noise(key_list[0], (TRACERS, LEV, NLAT, NLON), 1.0, 6.0, ((2, 8), (3, 4)), jnp.float32)
    wind_east = jnp.clip(jax.random.uniform(key_list[1], (LEV, NLAT, NLON), jnp.float32, -0.45, 0.45) * block_scale(key_list[1], (LEV, NLAT, NLON), ((1, 8), (2, 4)), -0.4, 0.0), -0.45, 0.45)
    wind_north = jnp.clip(jax.random.uniform(key_list[2], (LEV, NLAT, NLON), jnp.float32, -0.45, 0.45) * block_scale(key_list[2], (LEV, NLAT, NLON), ((1, 8), (2, 4)), -0.4, 0.0), -0.45, 0.45)
    polar_mask = draw_polar_mask(jax.random.fold_in(key_list[8], 71), 0)
    obs_owner_keys = jax.random.split(jax.random.fold_in(key_list[4], 1), NOBS // OBS_DEV)
    obs_owner_turns = jax.random.permutation(jax.random.fold_in(key_list[4], 3), NOBS // OBS_DEV)
    obs_owner = jax.vmap(lambda own, number: routed_block(jax.random.fold_in(key_list[4], 2), own, number, OBS_DEV, DEVICES, 1, CAP, 2))(obs_owner_keys, obs_owner_turns).reshape((NOBS, 1))
    obs_cell = set_ends(jax.random.randint(key_list[5], (NOBS,), 0, LAT_DEV * LON_DEV), jax.random.fold_in(key_list[5], 1), 0, (LAT_DEV * LON_DEV) - 1).astype(jnp.int32)
    obs_kernel = jnp.clip(jnp.exp(math.log(2.0) - 2.3025851 * jax.random.uniform(key_list[6], (NOBS, LEV), jnp.float32) ** block_scale(key_list[6], (NOBS, LEV), ((0, 32),), -0.2, 0.2)), 0.2, 2.0)
    obs_resid = noise(key_list[7], (NOBS, TRACERS), 1.0, 6.0, ((0, 32),), jnp.float32)
    return dict(adjoint_in=adjoint_in, wind_east=wind_east, wind_north=wind_north, polar_mask=polar_mask, obs_owner=obs_owner, obs_cell=obs_cell, obs_kernel=obs_kernel, obs_resid=obs_resid)


def route_forcing(adjoint_in, obs_owner, obs_cell, obs_kernel, obs_resid):
    lon_dev = NLON // N_LON
    owner_dev = obs_owner[:, 0]
    row_ids = (owner_dev // N_LON) * LAT_DEV + obs_cell // lon_dev
    col_ids = (owner_dev % N_LON) * lon_dev + obs_cell % lon_dev
    flat_index = (row_ids * NLON + col_ids).astype(jnp.int32)
    contrib = obs_resid[:, :, None] * obs_kernel[:, None, :]
    contrib = contrib.reshape(contrib.shape[0], TRACERS * LEV)
    adjoint = adjoint_in.reshape(TRACERS * LEV, NLAT * NLON)
    adjoint = adjoint.at[:, flat_index].add(contrib.T)
    return adjoint.reshape(TRACERS, LEV, NLAT, NLON)


def polar_filter(adjoint, polar_mask):
    row_ids = jnp.arange(NLAT)
    cosine = jnp.sin(math.pi * (row_ids + 0.5) / NLAT)
    lat_ratio = cosine / math.sin(math.pi * POLAR_MAX / NLAT)
    wavenum = jnp.arange(NLON // 2 + 1)
    sine_k = jnp.sin(math.pi * wavenum / NLON)
    damping = lat_ratio[:, None] / jnp.maximum(sine_k[None, :], lat_ratio[:, None])
    damping = jnp.where(polar_mask[:, None] > 0, damping, 1.0)
    spectra = jnp.fft.rfft(adjoint, axis=-1)
    return jnp.fft.irfft(spectra * damping[None, None], n=NLON, axis=-1)


def adjoint_advect(adjoint, wind_east, wind_north):
    row_ids = jnp.arange(NLAT)
    north_wind = jnp.where(row_ids[None, :, None] < NLAT - 1, wind_north, 0.0)
    east_face = jnp.maximum(wind_east, 0.0)
    west_face = jnp.minimum(jnp.roll(wind_east, 1, axis=-1), 0.0)
    north_face = jnp.maximum(north_wind, 0.0)
    south_wind = jnp.concatenate([jnp.zeros_like(north_wind[:, :1]), north_wind[:, :-1]], axis=1)
    south_face = jnp.minimum(south_wind, 0.0)
    east_val = jnp.roll(adjoint, -1, axis=-1)
    west_val = jnp.roll(adjoint, 1, axis=-1)
    zero_row = jnp.zeros_like(adjoint[:, :, :1])
    upper_val = jnp.concatenate([adjoint[:, :, 1:], zero_row], axis=2)
    lower_val = jnp.concatenate([zero_row, adjoint[:, :, :-1]], axis=2)
    result = adjoint + east_face * (east_val - adjoint) + west_face * (adjoint - west_val)
    return result + north_face * (upper_val - adjoint) + south_face * (adjoint - lower_val)


def reference(adjoint_in, wind_east, wind_north, polar_mask, obs_owner, obs_cell, obs_kernel, obs_resid):
    forced = route_forcing(adjoint_in, obs_owner, obs_cell, obs_kernel, obs_resid)
    filtered = polar_filter(forced, polar_mask)
    return adjoint_advect(filtered, wind_east, wind_north)
```

```python
import functools
import math

import jax
import jax.numpy as jnp
import ml_dtypes
import numpy as np
from jax import lax
from jax.experimental import pallas as pl
from jax.experimental.pallas import tpu as pltpu
from jax.sharding import PartitionSpec as P

MESH = pl.DeviceIdType.MESH
LANE_STEP = 256
ACCS = 4
UNROLL = 2


def circle_tables(lon_width):
    width = lon_width // 4
    half = width // 2

    def table(waves, turns, repeats):
        places = np.concatenate([np.arange(width) + width * turn for turn in range(repeats)])
        phase = 2.0 * np.pi * ((places[:, None] * waves[None, :]) % lon_width) / lon_width
        return np.cos(phase - 0.5 * np.pi * turns[None, :])

    zero = np.concatenate([4 * np.arange(half + 1), 4 * np.arange(1, half)])
    zero_turns = np.concatenate([np.zeros(half + 1), np.ones(half - 1)])
    zero_weights = np.where((zero == 0) | (zero == lon_width // 2), 1.0, 2.0)
    two = np.tile(4 * np.arange(half) + 2, 2)
    one = np.tile(4 * np.arange(width) + 1, 2)
    parts = [
        (table(zero, zero_turns, 1), zero, zero_weights / lon_width),
        (table(two, np.repeat([0, 1], half), 1), two, np.full(width, 2.0 / lon_width)),
        (table(one, np.repeat([0, 1], width), 2), one, np.full(2 * width, 2.0 / lon_width)),
    ]
    bases, waves, weights = [], [], []
    for basis, wave, weight in parts:
        extra = -wave.shape[0] % LANE_STEP
        basis = np.pad(basis, ((0, 0), (0, extra)))
        bases += [basis[i : i + width] for i in range(0, basis.shape[0], width)]
        waves.append(np.pad(wave, (0, extra)))
        weights.append(np.pad(weight, (0, extra)))
    basis = np.concatenate(bases, axis=1).astype(np.float32)
    high = basis.astype(ml_dtypes.bfloat16)
    low = (basis - high.astype(np.float32)).astype(ml_dtypes.bfloat16)
    return high, low, np.concatenate(waves), np.concatenate(weights)


def helper_bands(lat_count):
    if lat_count != 8:
        return {}
    return {0: (2, 4), lat_count - 1: (lat_count - 3, lat_count - 5)}


def damping_factors(polar_mask, band, lat_dev, total_rows, lon_width, waves, weights):
    rows = band * lat_dev + jnp.arange(lat_dev, dtype=jnp.int32)
    lat_ratio = jnp.sin(math.pi * (rows.astype(jnp.float32) + 0.5) / total_rows) / math.sin(
        math.pi * (total_rows // 8) / total_rows
    )
    live = lax.dynamic_slice_in_dim(polar_mask, band * lat_dev, lat_dev) > 0
    sine_k = jnp.asarray(np.sin(np.pi * waves / lon_width).astype(np.float32))
    damping = lat_ratio[:, None] / jnp.maximum(sine_k[None, :], lat_ratio[:, None])
    factor = (damping - 1.0) * jnp.asarray(weights.astype(np.float32))[None, :]
    return jnp.where(live[:, None], factor, 0.0)


def scatter_kernel(cells_ref, values_ref, out_ref, *extra):
    accs = (out_ref,) + extra
    total, width = out_ref.shape
    chunk = 64
    count = values_ref.shape[0]

    def clear(i, carry):
        where = pl.ds(pl.multiple_of(i * chunk, chunk), chunk)
        for acc in accs:
            acc[where, :] = jnp.zeros((chunk, width), jnp.float32)
        return carry

    lax.fori_loop(0, total // chunk, clear, 0)
    step = 8 * UNROLL

    def add(i, carry):
        for turn in range(UNROLL):
            base = pl.multiple_of(i * step + turn * 8, 8)
            block = values_ref[pl.ds(base, 8), :]
            for first in range(0, 8, ACCS):
                places = [cells_ref[base + first + lane] for lane in range(ACCS)]
                news = [
                    accs[lane][pl.ds(places[lane], 1), :] + block[first + lane : first + lane + 1, :]
                    for lane in range(ACCS)
                ]
                for lane in range(ACCS):
                    accs[lane][pl.ds(places[lane], 1), :] = news[lane]
        return carry

    lax.fori_loop(0, count // step, add, 0)

    def join(i, carry):
        where = pl.ds(pl.multiple_of(i * chunk, chunk), chunk)
        total_here = accs[0][where, :]
        for acc in extra:
            total_here = total_here + acc[where, :]
        out_ref[where, :] = total_here
        return carry

    lax.fori_loop(0, total // chunk, join, 0)


def place_kernel(slots_ref, payload_ref, out_ref):
    chunk = 64

    def clear(i, carry):
        where = pl.ds(pl.multiple_of(i * chunk, chunk), chunk)
        out_ref[where, :] = jnp.zeros((chunk, out_ref.shape[1]), jnp.float32)
        return carry

    lax.fori_loop(0, out_ref.shape[0] // chunk, clear, 0)

    def put(i, carry):
        base = pl.multiple_of(i * 16, 16)
        block = payload_ref[pl.ds(base, 16), :]
        slots = [slots_ref[base + j] for j in range(16)]
        for j, slot in enumerate(slots):
            out_ref[pl.ds(slot, 1), :] = block[j : j + 1, :]
        return carry

    lax.fori_loop(0, payload_ref.shape[0] // 16, put, 0)


def place_soundings(slots, payload, total):
    return pl.pallas_call(
        place_kernel,
        out_shape=jax.ShapeDtypeStruct((total, payload.shape[1]), jnp.float32),
        in_specs=[
            pl.BlockSpec(memory_space=pltpu.SMEM),
            pl.BlockSpec(memory_space=pltpu.VMEM),
        ],
        out_specs=pl.BlockSpec(memory_space=pltpu.VMEM),
        compiler_params=pltpu.CompilerParams(vmem_limit_bytes=32 * 1024 * 1024),
    )(slots, payload)


def add_soundings(cells, values, total):
    width = values.shape[1]
    return pl.pallas_call(
        scatter_kernel,
        out_shape=jax.ShapeDtypeStruct((total, width), jnp.float32),
        in_specs=[
            pl.BlockSpec(memory_space=pltpu.SMEM),
            pl.BlockSpec(memory_space=pltpu.VMEM),
        ],
        out_specs=pl.BlockSpec(memory_space=pltpu.VMEM),
        scratch_shapes=[pltpu.VMEM((total, width), jnp.float32)] * (ACCS - 1),
        compiler_params=pltpu.CompilerParams(vmem_limit_bytes=48 * 1024 * 1024),
    )(cells, values)


def level_step(levels):
    return 4 if levels % 4 == 0 else 1


def stencil_kernel(
    keep_ref, field_ref, east_ref, north_ref, lower_ref, upper_ref, right_ref, left_ref, out_ref,
    wide, edge,
):
    tracers, step, rows, width = field_ref.shape
    levels = upper_ref.shape[0] // tracers
    padded = wide.shape[1]
    lanes = lax.broadcasted_iota(jnp.int32, (rows, padded), 1)
    subs = lax.broadcasted_iota(jnp.int32, (rows, padded), 0)
    keep = keep_ref[0]
    first = pl.program_id(0) * step
    right = right_ref[0]
    left = left_ref[0]

    def widened(slot, block):
        wide[slot * rows : (slot + 1) * rows, 0:width] = block
        return wide[slot * rows : (slot + 1) * rows, :]

    for level in range(step):
        for tracer in range(tracers):
            place = tracer * levels + first + level
            edge[tracer : tracer + 1, 0:width] = upper_ref[pl.ds(place, 1), :]
            edge[tracers + tracer : tracers + tracer + 1, 0:width] = lower_ref[pl.ds(place, 1), :]
        edge[2 * tracers : 2 * tracers + 1, 0:width] = lower_ref[
            pl.ds(tracers * levels + first + level, 1), :
        ]
        lane = tracers * step + level
        wind_east = widened(0, east_ref[level])
        wind_west = jnp.where(
            lanes == 0, left[:, lane : lane + 1], pltpu.roll(wind_east, 1, 1)
        )
        wind_north = widened(1, north_ref[level])
        wind_south = jnp.where(
            subs == 0, edge[2 * tracers : 2 * tracers + 1, :], pltpu.roll(wind_north, 1, 0)
        )
        wind_north = jnp.where((subs == rows - 1) & (keep == 0), 0.0, wind_north)
        east_face = jnp.maximum(wind_east, 0.0)
        west_face = jnp.minimum(wind_west, 0.0)
        north_face = jnp.maximum(wind_north, 0.0)
        south_face = jnp.minimum(wind_south, 0.0)
        for tracer in range(tracers):
            other = tracers + tracer
            lane = tracer * step + level
            center = widened(2 + tracer, field_ref[tracer, level])
            east_val = jnp.where(
                lanes == width - 1, right[:, lane : lane + 1], pltpu.roll(center, padded - 1, 1)
            )
            west_val = jnp.where(lanes == 0, left[:, lane : lane + 1], pltpu.roll(center, 1, 1))
            upper_val = jnp.where(
                subs == rows - 1, edge[tracer : tracer + 1, :], pltpu.roll(center, rows - 1, 0)
            )
            lower_val = jnp.where(subs == 0, edge[other : other + 1, :], pltpu.roll(center, 1, 0))
            result = center + east_face * (east_val - center) + west_face * (center - west_val)
            result = result + north_face * (upper_val - center) + south_face * (center - lower_val)
            out_ref[tracer, level] = result[:, 0:width]


def advect(keep, field, wind_east, wind_north, lower, upper, right, left):
    tracers, levels, rows, width = field.shape
    step = level_step(levels)
    padded = -(-(width + 1) // 128) * 128

    def four(depth, span):
        return pl.BlockSpec((tracers, step, depth, span), lambda i: (0, i, 0, 0))

    def three(depth, span):
        return pl.BlockSpec((step, depth, span), lambda i: (i, 0, 0))

    def whole(array):
        return pl.BlockSpec(array.shape, lambda i: (0, 0))

    column = pl.BlockSpec((1, rows, 128), lambda i: (i, 0, 0))
    return pl.pallas_call(
        stencil_kernel,
        grid=(levels // step,),
        out_shape=jax.ShapeDtypeStruct(field.shape, jnp.float32),
        in_specs=[
            pl.BlockSpec(memory_space=pltpu.SMEM),
            four(rows, width), three(rows, width), three(rows, width),
            whole(lower), whole(upper), column, column,
        ],
        out_specs=four(rows, width),
        scratch_shapes=[
            pltpu.VMEM(((2 + tracers) * rows, padded), jnp.float32),
            pltpu.VMEM((8, padded), jnp.float32),
        ],
        compiler_params=pltpu.CompilerParams(vmem_limit_bytes=32 * 1024 * 1024),
    )(keep, field, wind_east, wind_north, lower, upper, right, left)


def circle_kernel(
    plan, x_ref, we_ref, wn_ref, fac_ref, high_hbm, low_hbm,
    filt_ref, lower_ref, upper_ref, right_ref, left_ref,
    recv, hold, high, low, pieces, spectra, low_out, up_out, right_out, left_out, wind_rows,
    wind_cols, local_sem, direct_send, direct_recv, out_send, out_recv, relay_send, relay_recv,
    back_send, back_recv, home_send, home_recv, edge_send, edge_recv,
):
    lats, lons, polar, helpers, share, counts, tracers, levels = plan
    fields, rows, lon_dev = x_ref.shape
    quarter = high.shape[0]
    blocks = quarter // lon_dev
    lat = lax.axis_index("lat")
    z = lax.axis_index("lon")
    groups = len(counts) - 1
    helper_of = [(h, p, g) for p in helpers for g, h in enumerate(helpers[p])]

    def among(choices):
        found = lat == choices[0]
        for choice in choices[1:]:
            found = found | (lat == choice)
        return found

    is_polar = among(polar)
    is_helper = among([h for h, _, _ in helper_of]) if helper_of else None

    def ahead(k):
        return lax.rem(z + k, lons)

    def behind(k):
        return lax.rem(z + lons - k, lons)

    bring = [
        pltpu.make_async_copy(high_hbm, high, local_sem.at[0]),
        pltpu.make_async_copy(low_hbm, low, local_sem.at[1]),
    ]
    for copy in bring:
        copy.start()
    lane0 = (lon_dev - 1) // 128 * 128
    winds = [
        pltpu.make_async_copy(wn_ref.at[:, pl.ds(rows - 8, 8), :], wind_rows, local_sem.at[2]),
        pltpu.make_async_copy(
            we_ref.at[:, :, pl.ds(lane0, lon_dev - lane0)], wind_cols, local_sem.at[3]
        ),
    ]
    for copy in winds:
        copy.start()

    barrier = pltpu.get_barrier_semaphore()

    def greet(where):
        pl.semaphore_signal(barrier, inc=1, device_id=where, device_id_type=MESH)

    @pl.when(lat > 0)
    def _():
        greet((lat - 1, z))

    @pl.when(lat < lats - 1)
    def _():
        greet((lat + 1, z))

    greet((lat, ahead(1)))
    greet((lat, behind(1)))
    expected = 2 + (lat > 0).astype(jnp.int32) + (lat < lats - 1).astype(jnp.int32)
    for band in polar:
        friends = helpers.get(band, ())

        @pl.when(lat == band)
        def _():
            for k in range(2, lons - 1):
                greet((lat, ahead(k)))
            for h in friends:
                for k in range(lons):
                    greet((h, ahead(k)))

        mine = (lat == band).astype(jnp.int32)
        expected = expected + mine * (lons - 3 + len(friends) * lons)
    for h, p, _ in helper_of:

        @pl.when(lat == h)
        def _():
            for k in range(2, lons - 1):
                greet((lat, ahead(k)))
            for k in range(lons):
                greet((p, ahead(k)))

        expected = expected + (lat == h).astype(jnp.int32) * (lons - 3 + lons)
    pl.semaphore_wait(barrier, expected)

    offsets = [sum(counts[:i]) for i in range(len(counts))]
    order = sorted(range(1, lons), key=lambda k: -min(k, lons - k))

    def remote(src, dst, send, took, where):
        return pltpu.make_async_remote_copy(
            src_ref=src, dst_ref=dst, send_sem=send, recv_sem=took,
            device_id=where, device_id_type=MESH,
        )

    def direct(k):
        return remote(
            x_ref.at[pl.ds(share * ahead(k), counts[0])], recv.at[z, pl.ds(0, counts[0])],
            direct_send.at[k], direct_recv.at[k], (lat, ahead(k)),
        )

    def outward(g, k, where):
        count = counts[1 + g]
        slot = recv.at[z, pl.ds(0, count)] if k == 0 else hold.at[ahead(k)]
        return remote(
            x_ref.at[pl.ds(share * ahead(k) + offsets[1 + g], count)], slot,
            out_send.at[g * lons + k], out_recv.at[k], (where, z),
        )

    def relay(k, count):
        return remote(
            hold.at[ahead(k)], recv.at[z, pl.ds(0, count)],
            relay_send.at[k], relay_recv.at[k], (lat, ahead(k)),
        )

    def back(k):
        return remote(
            recv.at[ahead(k), pl.ds(0, counts[0])], filt_ref.at[pl.ds(share * z, counts[0])],
            back_send.at[k], back_recv.at[k], (lat, ahead(k)),
        )

    def home(g, k, where):
        count = counts[1 + g]
        return remote(
            recv.at[ahead(k), pl.ds(0, count)],
            filt_ref.at[pl.ds(share * z + offsets[1 + g], count)],
            home_send.at[k], home_recv.at[g * lons + k], (where, ahead(k)),
        )

    def filter_share(count):
        depth = count * rows

        def quarter_of(i, f):
            held = [recv[i * blocks + j, f] for j in range(blocks)]
            return held[0] if blocks == 1 else jnp.concatenate(held, axis=1)

        for f in range(count):
            q = [quarter_of(i, f) for i in range(4)]
            even, odd = q[0] + q[2], q[1] + q[3]
            for p, part in enumerate((even + odd, even - odd, q[0] - q[2], q[1] - q[3])):
                top = part.astype(jnp.bfloat16)
                rest = (part - top.astype(jnp.float32)).astype(jnp.bfloat16)
                pieces[p, f * rows : (f + 1) * rows, :] = top
                pieces[p, depth + f * rows : depth + (f + 1) * rows, :] = rest

        single = high.shape[1] // 6
        spans = [(0, single), (single, 2 * single), (2 * single, 4 * single), (4 * single, 6 * single)]

        def forward(p):
            begin, end = spans[p]
            both = jnp.dot(
                pieces[p, 0 : 2 * depth, :], high[:, begin:end], preferred_element_type=jnp.float32
            )
            small = jnp.dot(
                pieces[p, 0:depth, :], low[:, begin:end], preferred_element_type=jnp.float32
            )
            return both[:depth] + both[depth:] + small

        def damped(values, begin):
            end = begin + values.shape[1]
            values = values.reshape(count, rows, end - begin) * fac_ref[:, begin:end][None]
            values = values.reshape(depth, end - begin)
            top = values.astype(jnp.bfloat16)
            spectra[0:depth, begin:end] = top
            spectra[depth : 2 * depth, begin:end] = (values - top.astype(jnp.float32)).astype(
                jnp.bfloat16
            )

        damped(forward(0), 0)
        damped(forward(1), single)
        damped(forward(2) + forward(3), 2 * single)

        def inverse(p):
            begin, end = spans[p]
            first = min(begin, 2 * single)
            last = first + end - begin
            sides = (((1,), (1,)), ((), ()))
            both = lax.dot_general(
                spectra[0 : 2 * depth, first:last], high[:, begin:end], sides,
                preferred_element_type=jnp.float32,
            )
            small = lax.dot_general(
                spectra[0:depth, first:last], low[:, begin:end], sides,
                preferred_element_type=jnp.float32,
            )
            return both[:depth] + both[depth:] + small

        zero_part, two_part = inverse(0), inverse(1)
        first, second = inverse(2), inverse(3)
        even_part, odd_part = zero_part + two_part, zero_part - two_part
        results = [even_part + first, odd_part + second, even_part - first, odd_part - second]
        for i in range(4):
            for j in range(blocks):
                change = results[i][:, j * lon_dev : (j + 1) * lon_dev]
                change = change.reshape(count, rows, lon_dev)
                place = i * blocks + j
                recv[place, 0:count] = recv[place, 0:count] + change

    for band in polar:
        friends = helpers.get(band, ())

        @pl.when(lat == band)
        def _():
            n0 = counts[0] if friends else share
            for k in order:
                for g, h in enumerate(friends):
                    outward(g, k, h).start()
                direct(k).start()
            for g, h in enumerate(friends):
                outward(g, 0, h).start()
            own = pltpu.make_async_copy(
                x_ref.at[pl.ds(share * z, n0)], recv.at[z, pl.ds(0, n0)], local_sem.at[4]
            )
            own.start()
            own.wait()
            for k in order:
                direct(k).wait_recv()
            for copy in bring:
                copy.wait()
            filter_share(n0)
            for k in order:
                back(k).start()
            mine = pltpu.make_async_copy(
                recv.at[z, pl.ds(0, n0)], filt_ref.at[pl.ds(share * z, n0)], local_sem.at[5]
            )
            mine.start()
            mine.wait()
            for k in order:
                direct(k).wait_send()
                back(k).wait_send()
                back(k).wait_recv()
            for g, h in enumerate(friends):
                for k in range(lons):
                    outward(g, k, h).wait_send()
                    home(g, k, h).wait_recv()

    for h, p, g in helper_of:

        @pl.when(lat == h)
        def _():
            for k in order:
                outward(g, k, p).wait_recv()
                relay(k, counts[1 + g]).start()
            outward(g, 0, p).wait_recv()
            for k in order:
                relay(k, counts[1 + g]).wait_recv()
            for copy in bring:
                copy.wait()
            filter_share(counts[1 + g])
            for k in order:
                home(g, k, p).start()
            home(g, 0, p).start()

    for copy in winds:
        copy.wait()

    @pl.when(jnp.logical_not(is_polar))
    def _():
        filt_ref[...] = x_ref[...]

    low_out[0:fields, :] = filt_ref[:, rows - 1, :]
    low_out[fields : fields + levels, :] = wind_rows[:, 7, :]
    up_out[...] = filt_ref[:, 0, :]

    def upward():
        return remote(low_out, lower_ref, edge_send.at[0], edge_recv.at[0], (lat + 1, z))

    def downward():
        return remote(up_out, upper_ref, edge_send.at[1], edge_recv.at[1], (lat - 1, z))

    @pl.when(lat < lats - 1)
    def _():
        upward().start()

    @pl.when(lat > 0)
    def _():
        downward().start()

    step = level_step(levels)
    lanes = lax.broadcasted_iota(jnp.int32, (rows, 128), 1)
    for i in range(levels // step):
        to_left = jnp.zeros((rows, 128), jnp.float32)
        to_right = jnp.zeros((rows, 128), jnp.float32)
        for level in range(step):
            for tracer in range(tracers):
                f = tracer * levels + i * step + level
                spot = lanes == tracer * step + level
                to_left = jnp.where(spot, filt_ref[f, :, 0:1], to_left)
                to_right = jnp.where(spot, filt_ref[f, :, lon_dev - 1 : lon_dev], to_right)
            column = wind_cols[i * step + level, :, lon_dev - 1 - lane0 : lon_dev - lane0]
            to_right = jnp.where(lanes == tracers * step + level, column, to_right)
        left_out[i] = to_left
        right_out[i] = to_right

    eastward = remote(right_out, left_ref, edge_send.at[2], edge_recv.at[2], (lat, ahead(1)))
    westward = remote(left_out, right_ref, edge_send.at[3], edge_recv.at[3], (lat, behind(1)))
    eastward.start()
    westward.start()

    @pl.when(lat == 0)
    def _():
        lower_ref[...] = jnp.zeros_like(lower_ref)

    @pl.when(lat == lats - 1)
    def _():
        upper_ref[...] = jnp.zeros_like(upper_ref)

    @pl.when(lat < lats - 1)
    def _():
        upward().wait_send()
        downward().wait_recv()

    @pl.when(lat > 0)
    def _():
        downward().wait_send()
        upward().wait_recv()

    eastward.wait()
    westward.wait()
    for h, p, g in helper_of:

        @pl.when(lat == h)
        def _():
            for k in order:
                relay(k, counts[1 + g]).wait_send()
                home(g, k, p).wait_send()
            home(g, 0, p).wait_send()

    quiet = jnp.logical_not(is_polar)
    if is_helper is not None:
        quiet = quiet & jnp.logical_not(is_helper)

    @pl.when(quiet)
    def _():
        for copy in bring:
            copy.wait()


def filter_circles(plan, x, wind_east, wind_north, factor, high, low):
    lats, lons, polar, helpers, share, counts, tracers, levels = plan
    fields, rows, lon_dev = x.shape
    quarter = high.shape[0]
    steps = levels // level_step(levels)
    lane0 = (lon_dev - 1) // 128 * 128
    depth = 2 * counts[0] * rows
    held = max(counts[1:]) if len(counts) > 1 else 1
    vmem = pl.BlockSpec(memory_space=pltpu.VMEM)
    hbm = pl.BlockSpec(memory_space=pl.ANY)
    f32 = jnp.float32
    groups = max(1, len(counts) - 1)
    column = (steps, rows, 128)
    return pl.pallas_call(
        functools.partial(circle_kernel, plan),
        out_shape=[
            jax.ShapeDtypeStruct(x.shape, f32),
            jax.ShapeDtypeStruct((fields + levels, lon_dev), f32),
            jax.ShapeDtypeStruct((fields, lon_dev), f32),
            jax.ShapeDtypeStruct(column, f32),
            jax.ShapeDtypeStruct(column, f32),
        ],
        in_specs=[vmem, hbm, hbm, vmem, hbm, hbm],
        out_specs=[vmem] * 5,
        scratch_shapes=[
            pltpu.VMEM((lons, counts[0], rows, lon_dev), f32),
            pltpu.VMEM((lons, held, rows, lon_dev), f32),
            pltpu.VMEM(high.shape, jnp.bfloat16),
            pltpu.VMEM(low.shape, jnp.bfloat16),
            pltpu.VMEM((4, depth, quarter), jnp.bfloat16),
            pltpu.VMEM((depth, factor.shape[1]), jnp.bfloat16),
            pltpu.VMEM((fields + levels, lon_dev), f32),
            pltpu.VMEM((fields, lon_dev), f32),
            pltpu.VMEM(column, f32),
            pltpu.VMEM(column, f32),
            pltpu.VMEM((levels, 8, lon_dev), f32),
            pltpu.VMEM((levels, rows, lon_dev - lane0), f32),
            pltpu.SemaphoreType.DMA((6,)),
            pltpu.SemaphoreType.DMA((lons,)),
            pltpu.SemaphoreType.DMA((lons,)),
            pltpu.SemaphoreType.DMA((groups * lons,)),
            pltpu.SemaphoreType.DMA((lons,)),
            pltpu.SemaphoreType.DMA((lons,)),
            pltpu.SemaphoreType.DMA((lons,)),
            pltpu.SemaphoreType.DMA((lons,)),
            pltpu.SemaphoreType.DMA((lons,)),
            pltpu.SemaphoreType.DMA((lons,)),
            pltpu.SemaphoreType.DMA((groups * lons,)),
            pltpu.SemaphoreType.DMA((4,)),
            pltpu.SemaphoreType.DMA((4,)),
        ],
        compiler_params=pltpu.CompilerParams(
            collective_id=1, has_side_effects=True, vmem_limit_bytes=56 * 1024 * 1024
        ),
    )(x, wind_east, wind_north, factor, high, low)


def owner_positions(owner_dev, devices):
    count = owner_dev.shape[0]
    span = 128
    one_hot = (owner_dev[:, None] == lax.broadcasted_iota(jnp.int32, (1, devices), 1)).astype(
        jnp.bfloat16
    ).reshape(count // span, span, devices)
    lower = jnp.asarray(np.tril(np.ones((span, span))), jnp.bfloat16)
    inner = jnp.einsum("ij,bjd->bid", lower, one_hot, preferred_element_type=jnp.float32)
    sums = inner[:, -1, :]
    blocks = count // span
    before = jnp.asarray(np.tril(np.ones((blocks, blocks)), -1), jnp.float32)
    offset = jnp.dot(before, sums, precision=lax.Precision.HIGHEST)
    ranks = (inner + offset[:, None, :]) * one_hot.astype(jnp.float32)
    return jnp.sum(ranks, axis=2).reshape(count).astype(jnp.int32) - 1


def shards(
    adjoint_in, wind_east, wind_north, polar_mask, obs_owner, obs_cell, obs_kernel, obs_resid
):
    tracers, levels, lat_dev, lon_dev = adjoint_in.shape
    fields = tracers * levels
    lat_count = lax.axis_size("lat")
    lon_count = lax.axis_size("lon")
    lat_index = lax.axis_index("lat")
    lon_width = lon_dev * lon_count
    total_rows = lat_dev * lat_count
    devices = lat_count * lon_count
    obs_count = obs_owner.shape[0]
    capacity = 2 * obs_count // devices

    owner_dev = obs_owner[:, 0]
    slot_index = owner_dev * capacity + owner_positions(owner_dev, devices)
    payload = jnp.concatenate(
        [
            obs_kernel,
            obs_resid,
            obs_cell.astype(jnp.float32)[:, None],
            jnp.zeros((obs_count, 32 - levels - tracers - 1), jnp.float32),
        ],
        axis=1,
    )
    send = place_soundings(slot_index, payload, devices * capacity)
    got = lax.all_to_all(
        send.reshape(devices, capacity, 32), ("lat", "lon"), split_axis=0, concat_axis=0, tiled=True
    ).reshape(devices * capacity, 32)
    got_cells = got[:, levels + tracers].astype(jnp.int32)
    got_values = (
        got[:, levels : levels + tracers, None] * got[:, None, :levels]
    ).reshape(devices * capacity, fields)
    forcing = add_soundings(got_cells, got_values, lat_dev * lon_dev)
    adjoint = (
        adjoint_in.reshape(fields, lat_dev, lon_dev)
        + forcing.T.reshape(fields, lat_dev, lon_dev)
    )

    high, low, waves, weights = circle_tables(lon_width)
    caps = -(-(total_rows // 8) // lat_dev)
    polar = sorted(set(range(caps)) | set(range(lat_count - caps, lat_count)))
    helpers = helper_bands(lat_count)
    share = fields // lon_count
    counts = (share // 2, share // 4, share // 4) if helpers else (share,)
    serves = np.arange(lat_count)
    for band, friends in helpers.items():
        serves[list(friends)] = band
    band = jnp.asarray(serves.astype(np.int32))[lat_index]
    factor = damping_factors(polar_mask, band, lat_dev, total_rows, lon_width, waves, weights)
    plan = (lat_count, lon_count, polar, helpers, share, counts, tracers, levels)
    field, lower, upper, right, left = filter_circles(
        plan, adjoint, wind_east, wind_north, factor, jnp.asarray(high), jnp.asarray(low)
    )
    field = field.reshape(tracers, levels, lat_dev, lon_dev)
    keep = (lat_index < lat_count - 1).astype(jnp.int32).reshape(1)
    return advect(keep, field, wind_east, wind_north, lower, upper, right, left)


def solution(mesh):
    placed = (
        P(None, None, "lat", "lon"),
        P(None, "lat", "lon"),
        P(None, "lat", "lon"),
        P(),
        P(("lat", "lon"), None),
        P(("lat", "lon")),
        P(("lat", "lon"), None),
        P(("lat", "lon"), None),
    )

    return jax.shard_map(
        shards, mesh=mesh, in_specs=placed, out_specs=P(None, None, "lat", "lon"), check_vma=False
    )
```

```python
import functools
import math

import jax
import jax.numpy as jnp
import ml_dtypes
import numpy as np
from jax import lax
from jax.experimental import pallas as pl
from jax.experimental.pallas import tpu as pltpu
from jax.sharding import PartitionSpec as P

MESH = pl.DeviceIdType.MESH
LANE_STEP = 256
WINDOW = 6


def circle_tables(lon_width):
    width = lon_width // 4
    half = width // 2

    def table(waves, turns, repeats):
        places = np.concatenate([np.arange(width) + width * turn for turn in range(repeats)])
        phase = 2.0 * np.pi * ((places[:, None] * waves[None, :]) % lon_width) / lon_width
        return np.cos(phase - 0.5 * np.pi * turns[None, :])

    zero = np.concatenate([4 * np.arange(half + 1), 4 * np.arange(1, half)])
    zero_turns = np.concatenate([np.zeros(half + 1), np.ones(half - 1)])
    zero_weights = np.where((zero == 0) | (zero == lon_width // 2), 1.0, 2.0)
    two = np.tile(4 * np.arange(half) + 2, 2)
    one = np.tile(4 * np.arange(width) + 1, 2)
    parts = [
        (table(zero, zero_turns, 1), zero, zero_weights / lon_width),
        (table(two, np.repeat([0, 1], half), 1), two, np.full(width, 2.0 / lon_width)),
        (table(one, np.repeat([0, 1], width), 2), one, np.full(2 * width, 2.0 / lon_width)),
    ]
    bases, waves, weights = [], [], []
    for basis, wave, weight in parts:
        extra = -wave.shape[0] % LANE_STEP
        basis = np.pad(basis, ((0, 0), (0, extra)))
        bases += [basis[i : i + width] for i in range(0, basis.shape[0], width)]
        waves.append(np.pad(wave, (0, extra)))
        weights.append(np.pad(weight, (0, extra)))
    basis = np.concatenate(bases, axis=1).astype(np.float32)
    high = basis.astype(ml_dtypes.bfloat16)
    low = (basis - high.astype(np.float32)).astype(ml_dtypes.bfloat16)
    return high, low, np.concatenate(waves), np.concatenate(weights)


def helper_bands(lat_count):
    if lat_count != 8:
        return {}
    return {0: (2, 4), lat_count - 1: (lat_count - 3, lat_count - 5)}


def damping_table(bands, lat_dev, total_rows, lon_width, waves, weights):
    rows = np.asarray(bands)[:, None] * lat_dev + np.arange(lat_dev)[None, :]
    lat_ratio = np.sin(np.pi * (rows + 0.5) / total_rows) / np.sin(
        np.pi * (total_rows // 8) / total_rows
    )
    sine_k = np.sin(np.pi * waves / lon_width)
    damping = lat_ratio[..., None] / np.maximum(sine_k, lat_ratio[..., None])
    return ((damping - 1.0) * weights).astype(np.float32)


def pack_layout(capacity, levels, tracers):
    halves = max(1, capacity // 128)
    rows = halves * (levels + tracers + 1)
    return halves, capacity // halves, rows + -rows % 8


def pack_kernel(levels, tracers, slots_ref, payload_ref, out_ref, placed):
    devices, _, width = out_ref.shape
    halves = placed.shape[0] // (devices * width)
    words = payload_ref.shape[1]
    chunk = 64

    def clear(i, carry):
        where = pl.ds(pl.multiple_of(i * chunk, chunk), chunk)
        placed[where, :] = jnp.zeros((chunk, placed.shape[1]), jnp.float32)
        return carry

    lax.fori_loop(0, placed.shape[0] // chunk, clear, 0)

    def put(i, carry):
        base = pl.multiple_of(i * 16, 16)
        block = payload_ref[pl.ds(base, 16), :]
        slots = [slots_ref[base + j] for j in range(16)]
        for j, slot in enumerate(slots):
            placed[pl.ds(slot, 1), 0:words] = block[j : j + 1, :]
        return carry

    lax.fori_loop(0, payload_ref.shape[0] // 16, put, 0)

    def turn(device, carry):
        for half in range(halves):
            base = pl.multiple_of((device * halves + half) * width, width)
            block = placed[pl.ds(base, width), :].T
            out_ref[device, half * levels : (half + 1) * levels, :] = block[0:levels]
            first = halves * levels + half * tracers
            out_ref[device, first : first + tracers, :] = block[levels : levels + tracers]
            first = halves * (levels + tracers) + half
            out_ref[device, first : first + 1, :] = block[levels + tracers : levels + tracers + 1]
        return carry

    lax.fori_loop(0, devices, turn, 0)


def pack_soundings(slots, payload, devices, capacity, levels, tracers):
    _, width, rows = pack_layout(capacity, levels, tracers)
    return pl.pallas_call(
        functools.partial(pack_kernel, levels, tracers),
        out_shape=jax.ShapeDtypeStruct((devices, rows, width), jnp.float32),
        in_specs=[
            pl.BlockSpec(memory_space=pltpu.SMEM),
            pl.BlockSpec(memory_space=pltpu.VMEM),
        ],
        out_specs=pl.BlockSpec(memory_space=pltpu.VMEM),
        scratch_shapes=[pltpu.VMEM((devices * capacity, 128), jnp.float32)],
        compiler_params=pltpu.CompilerParams(vmem_limit_bytes=32 * 1024 * 1024),
    )(slots, payload)


def force_kernel(
    plan, send_ref, x_hbm, out_ref, recv, total, turned, left0, left1, right0, right1, local_sem, send_sem, recv_sem
):
    lons, halves, levels, tracers, group = plan
    devices, _, width = send_ref.shape
    fields, rows, lon_dev = out_ref.shape
    me = lax.axis_index("lat") * lons + lax.axis_index("lon")
    start = pltpu.make_async_copy(x_hbm, out_ref, local_sem.at[0])
    start.start()
    own = pltpu.make_async_copy(send_ref.at[me], recv.at[me], local_sem.at[1])
    own.start()

    def ahead(k):
        return lax.rem(me + k, devices)

    def behind(k):
        return lax.rem(me + devices - k, devices)

    barrier = pltpu.get_barrier_semaphore()

    def greet(k, carry):
        other = ahead(k)
        pl.semaphore_signal(
            barrier, inc=1, device_id=(other // lons, lax.rem(other, lons)), device_id_type=MESH
        )
        return carry

    lax.fori_loop(1, devices, greet, 0)
    pl.semaphore_wait(barrier, devices - 1)

    def parcel(target, slot):
        return pltpu.make_async_remote_copy(
            src_ref=send_ref.at[target], dst_ref=recv.at[slot],
            send_sem=send_sem.at[target], recv_sem=recv_sem.at[slot],
            device_id=(target // lons, lax.rem(target, lons)), device_id_type=MESH,
        )

    steps = devices // group

    def each(step, act):
        for spot in reversed(range(group)):
            k = step * group + spot
            if spot == 0:

                @pl.when(k > 0)
                def _():
                    act(k)
            else:
                act(k)

    def post(step):
        each(step, lambda k: parcel(ahead(k), me).start())

    for step in range(min(WINDOW, steps)):
        post(step)

    columns = lax.broadcasted_iota(jnp.int32, (right0.shape[0], width), 0).astype(jnp.float32)
    depth = fields * rows

    def build(source, spot, left, right):
        for half in range(halves):
            lanes = slice((spot * halves + half) * width, (spot * halves + half + 1) * width)
            kernel = recv[source, half * levels : (half + 1) * levels, :]
            first = halves * (levels + tracers) + half
            cell = recv[source, first : first + 1, :]
            row = jnp.floor((cell + 0.5) * (1.0 / lon_dev))
            column = cell - row * lon_dev
            contrib = [
                kernel * recv[source, halves * levels + half * tracers + tracer, :][None, :]
                for tracer in range(tracers)
            ]
            contrib = jnp.concatenate(contrib, axis=0)
            top = contrib.astype(jnp.bfloat16)
            rest = (contrib - top.astype(jnp.float32)).astype(jnp.bfloat16)
            for place in range(rows):
                here = jnp.where(row == place, 1.0, 0.0)
                mask = jnp.broadcast_to(here, (16, width)).astype(jnp.bfloat16)
                mask = jnp.concatenate([mask] * (fields // 16), axis=0)
                f = place * fields
                left[f : f + fields, lanes] = top * mask
                left[depth + f : depth + f + fields, lanes] = rest * mask
            right[:, lanes] = jnp.where(columns == column, 1.0, 0.0).astype(jnp.bfloat16)

    def fetch(step):
        each(step, lambda k: parcel(behind(k), behind(k)).wait_recv())
        each(step, lambda k: parcel(ahead(k), me).wait_send())

        @pl.when(step + WINDOW < steps)
        def _():
            post(step + WINDOW)

    def multiply(left, right, first):
        columns = slice(first, first + LANE_STEP)
        product = lax.dot_general(
            left[...], right[columns, :], (((1,), (1,)), ((), ())),
            preferred_element_type=jnp.float32,
        )
        total[:, columns] += product[:depth] + product[depth:]

    def both(step, left, right, old_left, old_right):
        bands = list(range(0, old_right.shape[0], LANE_STEP))
        for spot in range(max(group, len(bands))):
            if spot < group:
                build(behind(step * group + spot), spot, left, right)
            if spot < len(bands):
                multiply(old_left, old_right, bands[spot])

    own.wait()
    total[...] = jnp.zeros_like(total)
    fetch(0)
    for spot in range(group):
        build(behind(spot), spot, left0, right0)

    def pair(i, carry):
        fetch(2 * i + 1)
        both(2 * i + 1, left1, right1, left0, right0)
        fetch(2 * i + 2)
        both(2 * i + 2, left0, right0, left1, right1)
        return carry

    lax.fori_loop(0, steps // 2 - 1, pair, 0)
    fetch(steps - 1)
    both(steps - 1, left1, right1, left0, right0)
    for first in range(0, right1.shape[0], LANE_STEP):
        multiply(left1, right1, first)
    start.wait()
    for first in range(0, lon_dev, 128):
        span = min(128, lon_dev - first)
        for place in range(rows):
            for f in range(0, fields, 8):
                turned[pl.ds(f * rows + place, 8, stride=rows), :] = total[
                    place * fields + f : place * fields + f + 8, first : first + 128
                ]
        out_ref[:, :, first : first + span] += turned[:, 0:span].reshape(fields, rows, span)


def force_field(send, x, lons, halves, levels, tracers):
    devices, rows, width = send.shape
    fields, lat_dev, lon_dev = x.shape
    group = max(1, 512 // (halves * width)) if width == 128 else 1
    span = group * halves * width
    left = pltpu.VMEM((2 * fields * lat_dev, span), jnp.bfloat16)
    right = pltpu.VMEM((lon_dev + -lon_dev % LANE_STEP, span), jnp.bfloat16)
    return pl.pallas_call(
        functools.partial(force_kernel, (lons, halves, levels, tracers, group)),
        out_shape=jax.ShapeDtypeStruct(x.shape, jnp.float32),
        in_specs=[pl.BlockSpec(memory_space=pltpu.VMEM), pl.BlockSpec(memory_space=pl.ANY)],
        out_specs=pl.BlockSpec(memory_space=pltpu.VMEM),
        scratch_shapes=[
            pltpu.VMEM(send.shape, jnp.float32),
            pltpu.VMEM((fields * lat_dev, right.shape[0]), jnp.float32),
            pltpu.VMEM((fields * lat_dev, 128), jnp.float32),
            left, left, right, right,
            pltpu.SemaphoreType.DMA((2,)),
            pltpu.SemaphoreType.DMA((devices,)),
            pltpu.SemaphoreType.DMA((devices,)),
        ],
        compiler_params=pltpu.CompilerParams(
            collective_id=2, has_side_effects=True, vmem_limit_bytes=56 * 1024 * 1024
        ),
    )(send, x)


def level_step(levels):
    return 4 if levels % 4 == 0 else 1


def stencil_kernel(
    keep_ref, field_ref, east_ref, north_ref, lower_ref, upper_ref, right_ref, left_ref, out_ref,
    wide, edge,
):
    tracers, step, rows, width = field_ref.shape
    levels = upper_ref.shape[0] // tracers
    padded = wide.shape[1]
    lanes = lax.broadcasted_iota(jnp.int32, (rows, padded), 1)
    subs = lax.broadcasted_iota(jnp.int32, (rows, padded), 0)
    keep = keep_ref[0]
    first = pl.program_id(0) * step
    right = right_ref[0]
    left = left_ref[0]

    def widened(slot, block):
        wide[slot * rows : (slot + 1) * rows, 0:width] = block
        return wide[slot * rows : (slot + 1) * rows, :]

    for level in range(step):
        for tracer in range(tracers):
            place = tracer * levels + first + level
            edge[tracer : tracer + 1, 0:width] = upper_ref[pl.ds(place, 1), :]
            edge[tracers + tracer : tracers + tracer + 1, 0:width] = lower_ref[pl.ds(place, 1), :]
        edge[2 * tracers : 2 * tracers + 1, 0:width] = lower_ref[
            pl.ds(tracers * levels + first + level, 1), :
        ]
        lane = tracers * step + level
        wind_east = widened(0, east_ref[level])
        wind_west = jnp.where(
            lanes == 0, left[:, lane : lane + 1], pltpu.roll(wind_east, 1, 1)
        )
        wind_north = widened(1, north_ref[level])
        wind_south = jnp.where(
            subs == 0, edge[2 * tracers : 2 * tracers + 1, :], pltpu.roll(wind_north, 1, 0)
        )
        wind_north = jnp.where((subs == rows - 1) & (keep == 0), 0.0, wind_north)
        east_face = jnp.maximum(wind_east, 0.0)
        west_face = jnp.minimum(wind_west, 0.0)
        north_face = jnp.maximum(wind_north, 0.0)
        south_face = jnp.minimum(wind_south, 0.0)
        for tracer in range(tracers):
            other = tracers + tracer
            lane = tracer * step + level
            center = widened(2 + tracer, field_ref[tracer, level])
            east_val = jnp.where(
                lanes == width - 1, right[:, lane : lane + 1], pltpu.roll(center, padded - 1, 1)
            )
            west_val = jnp.where(lanes == 0, left[:, lane : lane + 1], pltpu.roll(center, 1, 1))
            upper_val = jnp.where(
                subs == rows - 1, edge[tracer : tracer + 1, :], pltpu.roll(center, rows - 1, 0)
            )
            lower_val = jnp.where(subs == 0, edge[other : other + 1, :], pltpu.roll(center, 1, 0))
            result = center + east_face * (east_val - center) + west_face * (center - west_val)
            result = result + north_face * (upper_val - center) + south_face * (center - lower_val)
            out_ref[tracer, level] = result[:, 0:width]


def advect(keep, field, wind_east, wind_north, lower, upper, right, left):
    tracers, levels, rows, width = field.shape
    step = level_step(levels)
    padded = -(-(width + 1) // 128) * 128

    def four(depth, span):
        return pl.BlockSpec((tracers, step, depth, span), lambda i: (0, i, 0, 0))

    def three(depth, span):
        return pl.BlockSpec((step, depth, span), lambda i: (i, 0, 0))

    def whole(array):
        return pl.BlockSpec(array.shape, lambda i: (0, 0))

    column = pl.BlockSpec((1, rows, 128), lambda i: (i, 0, 0))
    return pl.pallas_call(
        stencil_kernel,
        grid=(levels // step,),
        out_shape=jax.ShapeDtypeStruct(field.shape, jnp.float32),
        in_specs=[
            pl.BlockSpec(memory_space=pltpu.SMEM),
            four(rows, width), three(rows, width), three(rows, width),
            whole(lower), whole(upper), column, column,
        ],
        out_specs=four(rows, width),
        scratch_shapes=[
            pltpu.VMEM(((2 + tracers) * rows, padded), jnp.float32),
            pltpu.VMEM((8, padded), jnp.float32),
        ],
        compiler_params=pltpu.CompilerParams(vmem_limit_bytes=60 * 1024 * 1024),
    )(keep, field, wind_east, wind_north, lower, upper, right, left)


def circle_kernel(
    plan, x_ref, we_ref, wn_ref, mask_ref, table_hbm, high_hbm, low_hbm,
    filt_ref, lower_ref, upper_ref, right_ref, left_ref,
    recv, hold, fac_ref, high, low, pieces, spectra, low_out, up_out, right_out, left_out, wind_rows,
    wind_cols, local_sem, direct_send, direct_recv, out_send, out_recv, relay_send, relay_recv,
    back_send, back_recv, home_send, home_recv, edge_send, edge_recv,
):
    lats, lons, polar, helpers, share, counts, tracers, levels = plan
    fields, rows, lon_dev = x_ref.shape
    quarter = high.shape[0]
    blocks = quarter // lon_dev
    lat = lax.axis_index("lat")
    z = lax.axis_index("lon")
    groups = len(counts) - 1
    helper_of = [(h, p, g) for p in helpers for g, h in enumerate(helpers[p])]

    def among(choices):
        found = lat == choices[0]
        for choice in choices[1:]:
            found = found | (lat == choice)
        return found

    is_polar = among(polar)
    is_helper = among([h for h, _, _ in helper_of]) if helper_of else None

    def ahead(k):
        return lax.rem(z + k, lons)

    def behind(k):
        return lax.rem(z + lons - k, lons)

    bring = [
        pltpu.make_async_copy(high_hbm, high, local_sem.at[0]),
        pltpu.make_async_copy(low_hbm, low, local_sem.at[1]),
    ]
    for copy in bring:
        copy.start()
    lane0 = (lon_dev - 1) // 128 * 128
    winds = [
        pltpu.make_async_copy(wn_ref.at[:, pl.ds(rows - 8, 8), :], wind_rows, local_sem.at[2]),
        pltpu.make_async_copy(
            we_ref.at[:, :, pl.ds(lane0, lon_dev - lane0)], wind_cols, local_sem.at[3]
        ),
    ]
    for copy in winds:
        copy.start()

    barrier = pltpu.get_barrier_semaphore()

    def greet(where):
        pl.semaphore_signal(barrier, inc=1, device_id=where, device_id_type=MESH)

    @pl.when(lat > 0)
    def _():
        greet((lat - 1, z))

    @pl.when(lat < lats - 1)
    def _():
        greet((lat + 1, z))

    greet((lat, ahead(1)))
    greet((lat, behind(1)))
    expected = 2 + (lat > 0).astype(jnp.int32) + (lat < lats - 1).astype(jnp.int32)
    for band in polar:
        friends = helpers.get(band, ())

        @pl.when(lat == band)
        def _():
            for k in range(2, lons - 1):
                greet((lat, ahead(k)))
            for h in friends:
                for k in range(lons):
                    greet((h, ahead(k)))

        mine = (lat == band).astype(jnp.int32)
        expected = expected + mine * (lons - 3 + len(friends) * lons)
    for h, p, _ in helper_of:

        @pl.when(lat == h)
        def _():
            for k in range(2, lons - 1):
                greet((lat, ahead(k)))
            for k in range(lons):
                greet((p, ahead(k)))

        expected = expected + (lat == h).astype(jnp.int32) * (lons - 3 + lons)
    pl.semaphore_wait(barrier, expected)

    offsets = [sum(counts[:i]) for i in range(len(counts))]
    order = sorted(range(1, lons), key=lambda k: -min(k, lons - k))

    def remote(src, dst, send, took, where):
        return pltpu.make_async_remote_copy(
            src_ref=src, dst_ref=dst, send_sem=send, recv_sem=took,
            device_id=where, device_id_type=MESH,
        )

    def direct(k):
        return remote(
            x_ref.at[pl.ds(share * ahead(k), counts[0])], recv.at[z, pl.ds(0, counts[0])],
            direct_send.at[k], direct_recv.at[k], (lat, ahead(k)),
        )

    def outward(g, k, where):
        count = counts[1 + g]
        slot = recv.at[z, pl.ds(0, count)] if k == 0 else hold.at[ahead(k)]
        return remote(
            x_ref.at[pl.ds(share * ahead(k) + offsets[1 + g], count)], slot,
            out_send.at[g * lons + k], out_recv.at[k], (where, z),
        )

    def relay(k, count):
        return remote(
            hold.at[ahead(k)], recv.at[z, pl.ds(0, count)],
            relay_send.at[k], relay_recv.at[k], (lat, ahead(k)),
        )

    def back(k):
        return remote(
            recv.at[ahead(k), pl.ds(0, counts[0])], filt_ref.at[pl.ds(share * z, counts[0])],
            back_send.at[k], back_recv.at[k], (lat, ahead(k)),
        )

    def home(g, k, where):
        count = counts[1 + g]
        return remote(
            recv.at[ahead(k), pl.ds(0, count)],
            filt_ref.at[pl.ds(share * z + offsets[1 + g], count)],
            home_send.at[k], home_recv.at[g * lons + k], (where, ahead(k)),
        )

    def factors(band):
        return pltpu.make_async_copy(
            table_hbm.at[polar.index(band)], fac_ref, local_sem.at[6]
        )

    def filter_share(count, band):
        depth = count * rows
        factors(band).wait()
        subs = lax.broadcasted_iota(jnp.int32, (rows, 1), 0)
        live = jnp.zeros((rows, 1), jnp.float32)
        for row in range(rows):
            filtered = mask_ref[band * rows + row].astype(jnp.float32)
            live = jnp.where(subs == row, filtered, live)
        fac_ref[...] = fac_ref[...] * live

        def quarter_of(i, f):
            held = [recv[i * blocks + j, f] for j in range(blocks)]
            return held[0] if blocks == 1 else jnp.concatenate(held, axis=1)

        for f in range(count):
            q = [quarter_of(i, f) for i in range(4)]
            even, odd = q[0] + q[2], q[1] + q[3]
            for p, part in enumerate((even + odd, even - odd, q[0] - q[2], q[1] - q[3])):
                top = part.astype(jnp.bfloat16)
                rest = (part - top.astype(jnp.float32)).astype(jnp.bfloat16)
                pieces[p, f * rows : (f + 1) * rows, :] = top
                pieces[p, depth + f * rows : depth + (f + 1) * rows, :] = rest

        single = high.shape[1] // 6
        spans = [(0, single), (single, 2 * single), (2 * single, 4 * single), (4 * single, 6 * single)]

        def forward(p):
            begin, end = spans[p]
            both = jnp.dot(
                pieces[p, 0 : 2 * depth, :], high[:, begin:end], preferred_element_type=jnp.float32
            )
            small = jnp.dot(
                pieces[p, 0:depth, :], low[:, begin:end], preferred_element_type=jnp.float32
            )
            return both[:depth] + both[depth:] + small

        def damped(values, begin):
            end = begin + values.shape[1]
            values = values.reshape(count, rows, end - begin) * fac_ref[:, begin:end][None]
            values = values.reshape(depth, end - begin)
            top = values.astype(jnp.bfloat16)
            spectra[0:depth, begin:end] = top
            spectra[depth : 2 * depth, begin:end] = (values - top.astype(jnp.float32)).astype(
                jnp.bfloat16
            )

        damped(forward(0), 0)
        damped(forward(1), single)
        damped(forward(2) + forward(3), 2 * single)

        def inverse(p):
            begin, end = spans[p]
            first = min(begin, 2 * single)
            last = first + end - begin
            sides = (((1,), (1,)), ((), ()))
            both = lax.dot_general(
                spectra[0 : 2 * depth, first:last], high[:, begin:end], sides,
                preferred_element_type=jnp.float32,
            )
            small = lax.dot_general(
                spectra[0:depth, first:last], low[:, begin:end], sides,
                preferred_element_type=jnp.float32,
            )
            return both[:depth] + both[depth:] + small

        zero_part, two_part = inverse(0), inverse(1)
        first, second = inverse(2), inverse(3)
        even_part, odd_part = zero_part + two_part, zero_part - two_part
        results = [even_part + first, odd_part + second, even_part - first, odd_part - second]
        for i in range(4):
            for j in range(blocks):
                change = results[i][:, j * lon_dev : (j + 1) * lon_dev]
                change = change.reshape(count, rows, lon_dev)
                place = i * blocks + j
                recv[place, 0:count] = recv[place, 0:count] + change

    for band in polar:
        friends = helpers.get(band, ())

        @pl.when(lat == band)
        def _():
            n0 = counts[0] if friends else share
            factors(band).start()
            for k in order:
                for g, h in enumerate(friends):
                    outward(g, k, h).start()
                direct(k).start()
            for g, h in enumerate(friends):
                outward(g, 0, h).start()
            own = pltpu.make_async_copy(
                x_ref.at[pl.ds(share * z, n0)], recv.at[z, pl.ds(0, n0)], local_sem.at[4]
            )
            own.start()
            own.wait()
            for k in order:
                direct(k).wait_recv()
            for copy in bring:
                copy.wait()
            filter_share(n0, band)
            for k in order:
                back(k).start()
            mine = pltpu.make_async_copy(
                recv.at[z, pl.ds(0, n0)], filt_ref.at[pl.ds(share * z, n0)], local_sem.at[5]
            )
            mine.start()
            mine.wait()
            for k in order:
                direct(k).wait_send()
                back(k).wait_send()
                back(k).wait_recv()
            for g, h in enumerate(friends):
                for k in range(lons):
                    outward(g, k, h).wait_send()
                    home(g, k, h).wait_recv()

    for h, p, g in helper_of:

        @pl.when(lat == h)
        def _():
            factors(p).start()
            for k in order:
                outward(g, k, p).wait_recv()
                relay(k, counts[1 + g]).start()
            outward(g, 0, p).wait_recv()
            for k in order:
                relay(k, counts[1 + g]).wait_recv()
            for copy in bring:
                copy.wait()
            filter_share(counts[1 + g], p)
            for k in order:
                home(g, k, p).start()
            home(g, 0, p).start()

    for copy in winds:
        copy.wait()

    @pl.when(jnp.logical_not(is_polar))
    def _():
        filt_ref[...] = x_ref[...]

    low_out[0:fields, :] = filt_ref[:, rows - 1, :]
    low_out[fields : fields + levels, :] = wind_rows[:, 7, :]
    up_out[...] = filt_ref[:, 0, :]

    def upward():
        return remote(low_out, lower_ref, edge_send.at[0], edge_recv.at[0], (lat + 1, z))

    def downward():
        return remote(up_out, upper_ref, edge_send.at[1], edge_recv.at[1], (lat - 1, z))

    @pl.when(lat < lats - 1)
    def _():
        upward().start()

    @pl.when(lat > 0)
    def _():
        downward().start()

    step = level_step(levels)
    lanes = lax.broadcasted_iota(jnp.int32, (rows, 128), 1)
    for i in range(levels // step):
        to_left = jnp.zeros((rows, 128), jnp.float32)
        to_right = jnp.zeros((rows, 128), jnp.float32)
        for level in range(step):
            for tracer in range(tracers):
                f = tracer * levels + i * step + level
                spot = lanes == tracer * step + level
                to_left = jnp.where(spot, filt_ref[f, :, 0:1], to_left)
                to_right = jnp.where(spot, filt_ref[f, :, lon_dev - 1 : lon_dev], to_right)
            column = wind_cols[i * step + level, :, lon_dev - 1 - lane0 : lon_dev - lane0]
            to_right = jnp.where(lanes == tracers * step + level, column, to_right)
        left_out[i] = to_left
        right_out[i] = to_right

    eastward = remote(right_out, left_ref, edge_send.at[2], edge_recv.at[2], (lat, ahead(1)))
    westward = remote(left_out, right_ref, edge_send.at[3], edge_recv.at[3], (lat, behind(1)))
    eastward.start()
    westward.start()

    @pl.when(lat == 0)
    def _():
        lower_ref[...] = jnp.zeros_like(lower_ref)

    @pl.when(lat == lats - 1)
    def _():
        upper_ref[...] = jnp.zeros_like(upper_ref)

    @pl.when(lat < lats - 1)
    def _():
        upward().wait_send()
        downward().wait_recv()

    @pl.when(lat > 0)
    def _():
        downward().wait_send()
        upward().wait_recv()

    eastward.wait()
    westward.wait()
    for h, p, g in helper_of:

        @pl.when(lat == h)
        def _():
            for k in order:
                relay(k, counts[1 + g]).wait_send()
                home(g, k, p).wait_send()
            home(g, 0, p).wait_send()

    quiet = jnp.logical_not(is_polar)
    if is_helper is not None:
        quiet = quiet & jnp.logical_not(is_helper)

    @pl.when(quiet)
    def _():
        for copy in bring:
            copy.wait()


def filter_circles(plan, x, wind_east, wind_north, polar_mask, table, high, low):
    _, lons, _, _, _, counts, tracers, levels = plan
    fields, rows, lon_dev = x.shape
    quarter = high.shape[0]
    steps = levels // level_step(levels)
    lane0 = (lon_dev - 1) // 128 * 128
    depth = 2 * counts[0] * rows
    held = max(counts[1:]) if len(counts) > 1 else 1
    vmem = pl.BlockSpec(memory_space=pltpu.VMEM)
    hbm = pl.BlockSpec(memory_space=pl.ANY)
    f32 = jnp.float32
    groups = max(1, len(counts) - 1)
    column = (steps, rows, 128)
    return pl.pallas_call(
        functools.partial(circle_kernel, plan),
        out_shape=[
            jax.ShapeDtypeStruct(x.shape, f32),
            jax.ShapeDtypeStruct((fields + levels, lon_dev), f32),
            jax.ShapeDtypeStruct((fields, lon_dev), f32),
            jax.ShapeDtypeStruct(column, f32),
            jax.ShapeDtypeStruct(column, f32),
        ],
        in_specs=[
            vmem, hbm, hbm, pl.BlockSpec(memory_space=pltpu.SMEM), hbm, hbm, hbm,
        ],
        out_specs=[vmem] * 5,
        scratch_shapes=[
            pltpu.VMEM((lons, counts[0], rows, lon_dev), f32),
            pltpu.VMEM((lons, held, rows, lon_dev), f32),
            pltpu.VMEM(table.shape[1:], f32),
            pltpu.VMEM(high.shape, jnp.bfloat16),
            pltpu.VMEM(low.shape, jnp.bfloat16),
            pltpu.VMEM((4, depth, quarter), jnp.bfloat16),
            pltpu.VMEM((depth, table.shape[2]), jnp.bfloat16),
            pltpu.VMEM((fields + levels, lon_dev), f32),
            pltpu.VMEM((fields, lon_dev), f32),
            pltpu.VMEM(column, f32),
            pltpu.VMEM(column, f32),
            pltpu.VMEM((levels, 8, lon_dev), f32),
            pltpu.VMEM((levels, rows, lon_dev - lane0), f32),
            pltpu.SemaphoreType.DMA((7,)),
            pltpu.SemaphoreType.DMA((lons,)),
            pltpu.SemaphoreType.DMA((lons,)),
            pltpu.SemaphoreType.DMA((groups * lons,)),
            pltpu.SemaphoreType.DMA((lons,)),
            pltpu.SemaphoreType.DMA((lons,)),
            pltpu.SemaphoreType.DMA((lons,)),
            pltpu.SemaphoreType.DMA((lons,)),
            pltpu.SemaphoreType.DMA((lons,)),
            pltpu.SemaphoreType.DMA((lons,)),
            pltpu.SemaphoreType.DMA((groups * lons,)),
            pltpu.SemaphoreType.DMA((4,)),
            pltpu.SemaphoreType.DMA((4,)),
        ],
        compiler_params=pltpu.CompilerParams(
            collective_id=1, has_side_effects=True, vmem_limit_bytes=56 * 1024 * 1024
        ),
    )(x, wind_east, wind_north, polar_mask, table, high, low)


def owner_positions(owner_dev, devices):
    count = owner_dev.shape[0]
    span = 128
    one_hot = (owner_dev[:, None] == lax.broadcasted_iota(jnp.int32, (1, devices), 1)).astype(
        jnp.bfloat16
    ).reshape(count // span, span, devices)
    lower = jnp.asarray(np.tril(np.ones((span, span))), jnp.bfloat16)
    inner = jnp.einsum("ij,bjd->bid", lower, one_hot, preferred_element_type=jnp.float32)
    sums = inner[:, -1, :]
    blocks = count // span
    before = jnp.asarray(np.tril(np.ones((blocks, blocks)), -1), jnp.float32)
    offset = jnp.dot(before, sums, precision=lax.Precision.HIGHEST)
    ranks = (inner + offset[:, None, :]) * one_hot.astype(jnp.float32)
    return jnp.sum(ranks, axis=2).reshape(count).astype(jnp.int32) - 1


def shards(
    adjoint_in, wind_east, wind_north, polar_mask, obs_owner, obs_cell, obs_kernel, obs_resid
):
    tracers, levels, lat_dev, lon_dev = adjoint_in.shape
    fields = tracers * levels
    lat_count = lax.axis_size("lat")
    lon_count = lax.axis_size("lon")
    lat_index = lax.axis_index("lat")
    lon_width = lon_dev * lon_count
    total_rows = lat_dev * lat_count
    devices = lat_count * lon_count
    obs_count = obs_owner.shape[0]
    capacity = 2 * obs_count // devices

    owner_dev = obs_owner[:, 0]
    slot_index = owner_dev * capacity + owner_positions(owner_dev, devices)
    payload = jnp.concatenate(
        [
            obs_kernel,
            obs_resid,
            obs_cell.astype(jnp.float32)[:, None],
            jnp.zeros((obs_count, 32 - levels - tracers - 1), jnp.float32),
        ],
        axis=1,
    )
    halves, _, _ = pack_layout(capacity, levels, tracers)
    send = pack_soundings(slot_index, payload, devices, capacity, levels, tracers)
    adjoint = force_field(
        send, adjoint_in.reshape(fields, lat_dev, lon_dev), lon_count, halves, levels, tracers
    )
    high, low, waves, weights = circle_tables(lon_width)
    caps = -(-(total_rows // 8) // lat_dev)
    polar = sorted(set(range(caps)) | set(range(lat_count - caps, lat_count)))
    helpers = helper_bands(lat_count)
    share = fields // lon_count
    counts = (share // 2, share // 4, share // 4) if helpers else (share,)
    table = damping_table(polar, lat_dev, total_rows, lon_width, waves, weights)
    plan = (lat_count, lon_count, polar, helpers, share, counts, tracers, levels)
    field, lower, upper, right, left = filter_circles(
        plan, adjoint, wind_east, wind_north, polar_mask, jnp.asarray(table), jnp.asarray(high),
        jnp.asarray(low),
    )
    field = field.reshape(tracers, levels, lat_dev, lon_dev)
    keep = (lat_index < lat_count - 1).astype(jnp.int32).reshape(1)
    return advect(keep, field, wind_east, wind_north, lower, upper, right, left)


def solution(mesh):
    placed = (
        P(None, None, "lat", "lon"),
        P(None, "lat", "lon"),
        P(None, "lat", "lon"),
        P(),
        P(("lat", "lon"), None),
        P(("lat", "lon")),
        P(("lat", "lon"), None),
        P(("lat", "lon"), None),
    )

    return jax.shard_map(
        shards, mesh=mesh, in_specs=placed, out_specs=P(None, None, "lat", "lon"), check_vma=False
    )
```

```python
import functools
import math

import jax
import jax.numpy as jnp
import ml_dtypes
import numpy as np
from jax import lax
from jax.experimental import pallas as pl
from jax.experimental.pallas import tpu as pltpu
from jax.sharding import PartitionSpec as P

MESH = pl.DeviceIdType.MESH
LANE_STEP = 256
WINDOW = 4


def circle_tables(lon_width):
    width = lon_width // 4
    half = width // 2

    def table(waves, turns, repeats):
        places = np.concatenate([np.arange(width) + width * turn for turn in range(repeats)])
        phase = 2.0 * np.pi * ((places[:, None] * waves[None, :]) % lon_width) / lon_width
        return np.cos(phase - 0.5 * np.pi * turns[None, :])

    zero = np.concatenate([4 * np.arange(half + 1), 4 * np.arange(1, half)])
    zero_turns = np.concatenate([np.zeros(half + 1), np.ones(half - 1)])
    zero_weights = np.where((zero == 0) | (zero == lon_width // 2), 1.0, 2.0)
    two = np.tile(4 * np.arange(half) + 2, 2)
    one = np.tile(4 * np.arange(width) + 1, 2)
    parts = [
        (table(zero, zero_turns, 1), zero, zero_weights / lon_width),
        (table(two, np.repeat([0, 1], half), 1), two, np.full(width, 2.0 / lon_width)),
        (table(one, np.repeat([0, 1], width), 2), one, np.full(2 * width, 2.0 / lon_width)),
    ]
    bases, waves, weights = [], [], []
    for basis, wave, weight in parts:
        extra = -wave.shape[0] % LANE_STEP
        basis = np.pad(basis, ((0, 0), (0, extra)))
        bases += [basis[i : i + width] for i in range(0, basis.shape[0], width)]
        waves.append(np.pad(wave, (0, extra)))
        weights.append(np.pad(weight, (0, extra)))
    basis = np.concatenate(bases, axis=1).astype(np.float32)
    high = basis.astype(ml_dtypes.bfloat16)
    low = (basis - high.astype(np.float32)).astype(ml_dtypes.bfloat16)
    return high, low, np.concatenate(waves), np.concatenate(weights)


def helper_bands(lat_count):
    if lat_count != 8:
        return {}
    return {0: (2, 4), lat_count - 1: (lat_count - 3, lat_count - 5)}


def damping_table(bands, lat_dev, total_rows, lon_width, waves, weights):
    rows = np.asarray(bands)[:, None] * lat_dev + np.arange(lat_dev)[None, :]
    lat_ratio = np.sin(np.pi * (rows + 0.5) / total_rows) / np.sin(
        np.pi * (total_rows // 8) / total_rows
    )
    sine_k = np.sin(np.pi * waves / lon_width)
    damping = lat_ratio[..., None] / np.maximum(sine_k, lat_ratio[..., None])
    return ((damping - 1.0) * weights).astype(np.float32)


def pack_layout(capacity, levels, tracers):
    halves = max(1, capacity // 128)
    rows = halves * (levels + tracers + 1)
    return halves, capacity // halves, rows + -rows % 8


def pack_kernel(levels, tracers, slots_ref, payload_ref, out_ref, placed):
    devices, _, width = out_ref.shape
    halves = placed.shape[0] // (devices * width)
    words = payload_ref.shape[1]
    chunk = 64

    def clear(i, carry):
        where = pl.ds(pl.multiple_of(i * chunk, chunk), chunk)
        placed[where, :] = jnp.zeros((chunk, placed.shape[1]), jnp.float32)
        return carry

    lax.fori_loop(0, placed.shape[0] // chunk, clear, 0)

    def put(i, carry):
        base = pl.multiple_of(i * 16, 16)
        block = payload_ref[pl.ds(base, 16), :]
        slots = [slots_ref[base + j] for j in range(16)]
        for j, slot in enumerate(slots):
            placed[pl.ds(slot, 1), 0:words] = block[j : j + 1, :]
        return carry

    lax.fori_loop(0, payload_ref.shape[0] // 16, put, 0)

    def turn(device, carry):
        for half in range(halves):
            base = pl.multiple_of((device * halves + half) * width, width)
            block = placed[pl.ds(base, width), :].T
            out_ref[device, half * levels : (half + 1) * levels, :] = block[0:levels]
            first = halves * levels + half * tracers
            out_ref[device, first : first + tracers, :] = block[levels : levels + tracers]
            first = halves * (levels + tracers) + half
            out_ref[device, first : first + 1, :] = block[levels + tracers : levels + tracers + 1]
        return carry

    lax.fori_loop(0, devices, turn, 0)


def pack_soundings(slots, payload, devices, capacity, levels, tracers):
    _, width, rows = pack_layout(capacity, levels, tracers)
    return pl.pallas_call(
        functools.partial(pack_kernel, levels, tracers),
        out_shape=jax.ShapeDtypeStruct((devices, rows, width), jnp.float32),
        in_specs=[
            pl.BlockSpec(memory_space=pltpu.SMEM),
            pl.BlockSpec(memory_space=pltpu.VMEM),
        ],
        out_specs=pl.BlockSpec(memory_space=pltpu.VMEM),
        scratch_shapes=[pltpu.VMEM((devices * capacity, 128), jnp.float32)],
        compiler_params=pltpu.CompilerParams(vmem_limit_bytes=32 * 1024 * 1024),
    )(slots, payload)


def force_kernel(
    plan, send_ref, x_hbm, out_ref, recv, total, turned, left0, left1, right0, right1, local_sem, send_sem, recv_sem
):
    lons, halves, levels, tracers, group = plan
    devices, _, width = send_ref.shape
    fields, rows, lon_dev = out_ref.shape
    me = lax.axis_index("lat") * lons + lax.axis_index("lon")
    start = pltpu.make_async_copy(x_hbm, out_ref, local_sem.at[0])
    start.start()
    own = pltpu.make_async_copy(send_ref.at[me], recv.at[me], local_sem.at[1])
    own.start()

    def ahead(k):
        return lax.rem(me + k, devices)

    def behind(k):
        return lax.rem(me + devices - k, devices)

    barrier = pltpu.get_barrier_semaphore()

    def greet(k, carry):
        other = ahead(k)
        pl.semaphore_signal(
            barrier, inc=1, device_id=(other // lons, lax.rem(other, lons)), device_id_type=MESH
        )
        return carry

    lax.fori_loop(1, devices, greet, 0)
    pl.semaphore_wait(barrier, devices - 1)

    def parcel(target, slot):
        return pltpu.make_async_remote_copy(
            src_ref=send_ref.at[target], dst_ref=recv.at[slot],
            send_sem=send_sem.at[target], recv_sem=recv_sem.at[slot],
            device_id=(target // lons, lax.rem(target, lons)), device_id_type=MESH,
        )

    steps = devices // group

    def each(step, act):
        for spot in reversed(range(group)):
            k = step * group + spot
            if spot == 0:

                @pl.when(k > 0)
                def _():
                    act(k)
            else:
                act(k)

    def post(step):
        each(step, lambda k: parcel(ahead(k), me).start())

    for step in range(min(WINDOW, steps)):
        post(step)

    columns = lax.broadcasted_iota(jnp.int32, (right0.shape[0], width), 0).astype(jnp.float32)
    depth = fields * rows

    def build(source, spot, left, right):
        for half in range(halves):
            lanes = slice((spot * halves + half) * width, (spot * halves + half + 1) * width)
            kernel = recv[source, half * levels : (half + 1) * levels, :]
            first = halves * (levels + tracers) + half
            cell = recv[source, first : first + 1, :]
            row = jnp.floor((cell + 0.5) * (1.0 / lon_dev))
            column = cell - row * lon_dev
            contrib = [
                kernel * recv[source, halves * levels + half * tracers + tracer, :][None, :]
                for tracer in range(tracers)
            ]
            contrib = jnp.concatenate(contrib, axis=0)
            top = contrib.astype(jnp.bfloat16)
            rest = (contrib - top.astype(jnp.float32)).astype(jnp.bfloat16)
            for place in range(rows):
                here = jnp.where(row == place, 1.0, 0.0)
                mask = jnp.broadcast_to(here, (16, width)).astype(jnp.bfloat16)
                mask = jnp.concatenate([mask] * (fields // 16), axis=0)
                f = place * fields
                left[f : f + fields, lanes] = top * mask
                left[depth + f : depth + f + fields, lanes] = rest * mask
            right[:, lanes] = jnp.where(columns == column, 1.0, 0.0).astype(jnp.bfloat16)

    def fetch(step):
        each(step, lambda k: parcel(behind(k), behind(k)).wait_recv())
        each(step, lambda k: parcel(ahead(k), me).wait_send())

        @pl.when(step + WINDOW < steps)
        def _():
            post(step + WINDOW)

    def multiply(left, right, first):
        columns = slice(first, first + LANE_STEP)
        product = lax.dot_general(
            left[...], right[columns, :], (((1,), (1,)), ((), ())),
            preferred_element_type=jnp.float32,
        )
        total[:, columns] += product[:depth] + product[depth:]

    def both(step, left, right, old_left, old_right):
        bands = list(range(0, old_right.shape[0], LANE_STEP))
        for spot in range(max(group, len(bands))):
            if spot < group:
                build(behind(step * group + spot), spot, left, right)
            if spot < len(bands):
                multiply(old_left, old_right, bands[spot])

    own.wait()
    total[...] = jnp.zeros_like(total)
    fetch(0)
    for spot in range(group):
        build(behind(spot), spot, left0, right0)

    def pair(i, carry):
        fetch(2 * i + 1)
        both(2 * i + 1, left1, right1, left0, right0)
        fetch(2 * i + 2)
        both(2 * i + 2, left0, right0, left1, right1)
        return carry

    lax.fori_loop(0, steps // 2 - 1, pair, 0)
    fetch(steps - 1)
    both(steps - 1, left1, right1, left0, right0)
    for first in range(0, right1.shape[0], LANE_STEP):
        multiply(left1, right1, first)
    start.wait()
    for first in range(0, lon_dev, 128):
        span = min(128, lon_dev - first)
        for place in range(rows):
            for f in range(0, fields, 8):
                turned[pl.ds(f * rows + place, 8, stride=rows), :] = total[
                    place * fields + f : place * fields + f + 8, first : first + 128
                ]
        out_ref[:, :, first : first + span] += turned[:, 0:span].reshape(fields, rows, span)


def level_step(levels):
    return 4 if levels % 4 == 0 else 1


def stencil_kernel(
    keep_ref, field_ref, east_ref, north_ref, lower_ref, south_ref, upper_ref, right_ref, left_ref, out_ref,
    wide, edge,
):
    tracers, step, rows, width = field_ref.shape
    levels = upper_ref.shape[0] // tracers
    padded = wide.shape[1]
    lanes = lax.broadcasted_iota(jnp.int32, (rows, padded), 1)
    subs = lax.broadcasted_iota(jnp.int32, (rows, padded), 0)
    keep = keep_ref[0]
    first = pl.program_id(0) * step
    right = right_ref[0]
    left = left_ref[0]

    def widened(slot, block):
        wide[slot * rows : (slot + 1) * rows, 0:width] = block
        return wide[slot * rows : (slot + 1) * rows, :]

    for level in range(step):
        for tracer in range(tracers):
            place = tracer * levels + first + level
            edge[tracer : tracer + 1, 0:width] = upper_ref[pl.ds(place, 1), :]
            edge[tracers + tracer : tracers + tracer + 1, 0:width] = lower_ref[pl.ds(place, 1), :]
        edge[2 * tracers : 2 * tracers + 1, 0:width] = south_ref[pl.ds(first + level, 1), :]
        lane = tracers * step + level
        wind_east = widened(0, east_ref[level])
        wind_west = jnp.where(
            lanes == 0, left[:, lane : lane + 1], pltpu.roll(wind_east, 1, 1)
        )
        wind_north = widened(1, north_ref[level])
        wind_south = jnp.where(
            subs == 0, edge[2 * tracers : 2 * tracers + 1, :], pltpu.roll(wind_north, 1, 0)
        )
        wind_north = jnp.where((subs == rows - 1) & (keep == 0), 0.0, wind_north)
        east_face = jnp.maximum(wind_east, 0.0)
        west_face = jnp.minimum(wind_west, 0.0)
        north_face = jnp.maximum(wind_north, 0.0)
        south_face = jnp.minimum(wind_south, 0.0)
        for tracer in range(tracers):
            other = tracers + tracer
            lane = tracer * step + level
            center = widened(2 + tracer, field_ref[tracer, level])
            east_val = jnp.where(
                lanes == width - 1, right[:, lane : lane + 1], pltpu.roll(center, padded - 1, 1)
            )
            west_val = jnp.where(lanes == 0, left[:, lane : lane + 1], pltpu.roll(center, 1, 1))
            upper_val = jnp.where(
                subs == rows - 1, edge[tracer : tracer + 1, :], pltpu.roll(center, rows - 1, 0)
            )
            lower_val = jnp.where(subs == 0, edge[other : other + 1, :], pltpu.roll(center, 1, 0))
            result = center + east_face * (east_val - center) + west_face * (center - west_val)
            result = result + north_face * (upper_val - center) + south_face * (center - lower_val)
            out_ref[tracer, level] = result[:, 0:width]


def advect(keep, field, wind_east, wind_north, lower, south, upper, right, left):
    tracers, levels, rows, width = field.shape
    step = level_step(levels)
    padded = -(-(width + 1) // 128) * 128

    def four(depth, span):
        return pl.BlockSpec((tracers, step, depth, span), lambda i: (0, i, 0, 0))

    def three(depth, span):
        return pl.BlockSpec((step, depth, span), lambda i: (i, 0, 0))

    def whole(array):
        return pl.BlockSpec(array.shape, lambda i: (0, 0))

    column = pl.BlockSpec((1, rows, 128), lambda i: (i, 0, 0))
    return pl.pallas_call(
        stencil_kernel,
        grid=(levels // step,),
        out_shape=jax.ShapeDtypeStruct(field.shape, jnp.float32),
        in_specs=[
            pl.BlockSpec(memory_space=pltpu.SMEM),
            four(rows, width), three(rows, width), three(rows, width),
            whole(lower), whole(south), whole(upper), column, column,
        ],
        out_specs=four(rows, width),
        scratch_shapes=[
            pltpu.VMEM(((2 + tracers) * rows, padded), jnp.float32),
            pltpu.VMEM((8, padded), jnp.float32),
        ],
        compiler_params=pltpu.CompilerParams(vmem_limit_bytes=60 * 1024 * 1024),
    )(keep, field, wind_east, wind_north, lower, south, upper, right, left)


def circle_kernel(
    plan, force, x_ref, we_ref, wn_ref, mask_ref, table_hbm, high_hbm, low_hbm,
    filt_ref, lower_ref, south_ref, upper_ref, right_ref, left_ref,
    recv, hold, fac_ref, high, low, pieces, spectra, low_out, south_out, up_out, right_out, left_out,
    wind_rows, wind_cols, local_sem, direct_send, direct_recv, out_send, out_recv, relay_send, relay_recv,
    back_send, back_recv, home_send, home_recv, edge_send, edge_recv,
):
    lats, lons, polar, helpers, share, counts, tracers, levels = plan
    fields, rows, lon_dev = x_ref.shape
    quarter = high.shape[0]
    blocks = quarter // lon_dev
    lat = lax.axis_index("lat")
    z = lax.axis_index("lon")
    groups = len(counts) - 1
    helper_of = [(h, p, g) for p in helpers for g, h in enumerate(helpers[p])]

    def among(choices):
        found = lat == choices[0]
        for choice in choices[1:]:
            found = found | (lat == choice)
        return found

    is_polar = among(polar)
    is_helper = among([h for h, _, _ in helper_of]) if helper_of else None

    def ahead(k):
        return lax.rem(z + k, lons)

    def behind(k):
        return lax.rem(z + lons - k, lons)

    bring = [
        pltpu.make_async_copy(high_hbm, high, local_sem.at[0]),
        pltpu.make_async_copy(low_hbm, low, local_sem.at[1]),
    ]
    for copy in bring:
        copy.start()
    lane0 = (lon_dev - 1) // 128 * 128
    winds = [
        pltpu.make_async_copy(wn_ref.at[:, pl.ds(rows - 8, 8), :], wind_rows, local_sem.at[2]),
        pltpu.make_async_copy(
            we_ref.at[:, :, pl.ds(lane0, lon_dev - lane0)], wind_cols, local_sem.at[3]
        ),
    ]
    for copy in winds:
        copy.start()

    force()

    offsets = [sum(counts[:i]) for i in range(len(counts))]
    order = sorted(range(1, lons), key=lambda k: -min(k, lons - k))

    def remote(src, dst, send, took, where):
        return pltpu.make_async_remote_copy(
            src_ref=src, dst_ref=dst, send_sem=send, recv_sem=took,
            device_id=where, device_id_type=MESH,
        )

    def direct(k):
        return remote(
            x_ref.at[pl.ds(share * ahead(k), counts[0])], recv.at[z, pl.ds(0, counts[0])],
            direct_send.at[k], direct_recv.at[k], (lat, ahead(k)),
        )

    def outward(g, k, where):
        count = counts[1 + g]
        slot = recv.at[z, pl.ds(0, count)] if k == 0 else hold.at[ahead(k)]
        return remote(
            x_ref.at[pl.ds(share * ahead(k) + offsets[1 + g], count)], slot,
            out_send.at[g * lons + k], out_recv.at[k], (where, z),
        )

    def relay(k, count):
        return remote(
            hold.at[ahead(k)], recv.at[z, pl.ds(0, count)],
            relay_send.at[k], relay_recv.at[k], (lat, ahead(k)),
        )

    def back(k):
        return remote(
            recv.at[ahead(k), pl.ds(0, counts[0])], filt_ref.at[pl.ds(share * z, counts[0])],
            back_send.at[k], back_recv.at[k], (lat, ahead(k)),
        )

    def home(g, k, where):
        count = counts[1 + g]
        return remote(
            recv.at[ahead(k), pl.ds(0, count)],
            filt_ref.at[pl.ds(share * z + offsets[1 + g], count)],
            home_send.at[k], home_recv.at[g * lons + k], (where, ahead(k)),
        )

    def factors(band):
        return pltpu.make_async_copy(
            table_hbm.at[polar.index(band)], fac_ref, local_sem.at[6]
        )

    def filter_share(count, band):
        depth = count * rows
        factors(band).wait()
        subs = lax.broadcasted_iota(jnp.int32, (rows, 1), 0)
        live = jnp.zeros((rows, 1), jnp.float32)
        for row in range(rows):
            filtered = mask_ref[band * rows + row].astype(jnp.float32)
            live = jnp.where(subs == row, filtered, live)
        fac_ref[...] = fac_ref[...] * live

        def quarter_of(i, f):
            held = [recv[i * blocks + j, f] for j in range(blocks)]
            return held[0] if blocks == 1 else jnp.concatenate(held, axis=1)

        for f in range(count):
            q = [quarter_of(i, f) for i in range(4)]
            even, odd = q[0] + q[2], q[1] + q[3]
            for p, part in enumerate((even + odd, even - odd, q[0] - q[2], q[1] - q[3])):
                top = part.astype(jnp.bfloat16)
                rest = (part - top.astype(jnp.float32)).astype(jnp.bfloat16)
                pieces[p, f * rows : (f + 1) * rows, :] = top
                pieces[p, depth + f * rows : depth + (f + 1) * rows, :] = rest

        single = high.shape[1] // 6
        spans = [(0, single), (single, 2 * single), (2 * single, 4 * single), (4 * single, 6 * single)]

        def forward(p):
            begin, end = spans[p]
            both = jnp.dot(
                pieces[p, 0 : 2 * depth, :], high[:, begin:end], preferred_element_type=jnp.float32
            )
            small = jnp.dot(
                pieces[p, 0:depth, :], low[:, begin:end], preferred_element_type=jnp.float32
            )
            return both[:depth] + both[depth:] + small

        def damped(values, begin):
            end = begin + values.shape[1]
            values = values.reshape(count, rows, end - begin) * fac_ref[:, begin:end][None]
            values = values.reshape(depth, end - begin)
            top = values.astype(jnp.bfloat16)
            spectra[0:depth, begin:end] = top
            spectra[depth : 2 * depth, begin:end] = (values - top.astype(jnp.float32)).astype(
                jnp.bfloat16
            )

        damped(forward(0), 0)
        damped(forward(1), single)
        damped(forward(2) + forward(3), 2 * single)

        def inverse(p):
            begin, end = spans[p]
            first = min(begin, 2 * single)
            last = first + end - begin
            sides = (((1,), (1,)), ((), ()))
            both = lax.dot_general(
                spectra[0 : 2 * depth, first:last], high[:, begin:end], sides,
                preferred_element_type=jnp.float32,
            )
            small = lax.dot_general(
                spectra[0:depth, first:last], low[:, begin:end], sides,
                preferred_element_type=jnp.float32,
            )
            return both[:depth] + both[depth:] + small

        zero_part, two_part = inverse(0), inverse(1)
        first, second = inverse(2), inverse(3)
        even_part, odd_part = zero_part + two_part, zero_part - two_part
        results = [even_part + first, odd_part + second, even_part - first, odd_part - second]
        for i in range(4):
            for j in range(blocks):
                change = results[i][:, j * lon_dev : (j + 1) * lon_dev]
                change = change.reshape(count, rows, lon_dev)
                place = i * blocks + j
                recv[place, 0:count] = recv[place, 0:count] + change

    def southward():
        return remote(south_out, south_ref, edge_send.at[4], edge_recv.at[4], (lat + 1, z))

    for copy in winds:
        copy.wait()
    south_out[...] = wind_rows[:, 7, :]

    @pl.when(lat < lats - 1)
    def _():
        southward().start()

    for band in polar:
        friends = helpers.get(band, ())

        @pl.when(lat == band)
        def _():
            n0 = counts[0] if friends else share
            factors(band).start()
            for k in order:
                direct(k).start()
            for k in order + [0]:
                for g, h in enumerate(friends):
                    outward(g, k, h).start()
                for g, h in enumerate(friends):
                    outward(g, k, h).wait_send()
            own = pltpu.make_async_copy(
                x_ref.at[pl.ds(share * z, n0)], recv.at[z, pl.ds(0, n0)], local_sem.at[4]
            )
            own.start()
            own.wait()
            for k in order:
                direct(k).wait_recv()
            for copy in bring:
                copy.wait()
            filter_share(n0, band)
            for k in order:
                back(k).start()
            mine = pltpu.make_async_copy(
                recv.at[z, pl.ds(0, n0)], filt_ref.at[pl.ds(share * z, n0)], local_sem.at[5]
            )
            mine.start()
            mine.wait()
            for k in order:
                direct(k).wait_send()
                back(k).wait_send()
                back(k).wait_recv()
            for g, h in enumerate(friends):
                for k in range(lons):
                    home(g, k, h).wait_recv()

    for h, p, g in helper_of:

        @pl.when(lat == h)
        def _():
            factors(p).start()
            for k in order:
                outward(g, k, p).wait_recv()
                relay(k, counts[1 + g]).start()
            outward(g, 0, p).wait_recv()
            for k in order:
                relay(k, counts[1 + g]).wait_recv()
            for copy in bring:
                copy.wait()
            filter_share(counts[1 + g], p)
            for k in order:
                home(g, k, p).start()
            home(g, 0, p).start()

    @pl.when(jnp.logical_not(is_polar))
    def _():
        filt_ref[...] = x_ref[...]

    low_out[...] = filt_ref[:, rows - 1, :]
    up_out[...] = filt_ref[:, 0, :]

    def upward():
        return remote(low_out, lower_ref, edge_send.at[0], edge_recv.at[0], (lat + 1, z))

    def downward():
        return remote(up_out, upper_ref, edge_send.at[1], edge_recv.at[1], (lat - 1, z))

    @pl.when(lat < lats - 1)
    def _():
        upward().start()

    @pl.when(lat > 0)
    def _():
        downward().start()

    step = level_step(levels)
    lanes = lax.broadcasted_iota(jnp.int32, (rows, 128), 1)
    for i in range(levels // step):
        to_left = jnp.zeros((rows, 128), jnp.float32)
        to_right = jnp.zeros((rows, 128), jnp.float32)
        for level in range(step):
            for tracer in range(tracers):
                f = tracer * levels + i * step + level
                spot = lanes == tracer * step + level
                to_left = jnp.where(spot, filt_ref[f, :, 0:1], to_left)
                to_right = jnp.where(spot, filt_ref[f, :, lon_dev - 1 : lon_dev], to_right)
            column = wind_cols[i * step + level, :, lon_dev - 1 - lane0 : lon_dev - lane0]
            to_right = jnp.where(lanes == tracers * step + level, column, to_right)
        left_out[i] = to_left
        right_out[i] = to_right

    eastward = remote(right_out, left_ref, edge_send.at[2], edge_recv.at[2], (lat, ahead(1)))
    westward = remote(left_out, right_ref, edge_send.at[3], edge_recv.at[3], (lat, behind(1)))
    eastward.start()
    westward.start()

    @pl.when(lat == 0)
    def _():
        lower_ref[...] = jnp.zeros_like(lower_ref)
        south_ref[...] = jnp.zeros_like(south_ref)

    @pl.when(lat == lats - 1)
    def _():
        upper_ref[...] = jnp.zeros_like(upper_ref)

    @pl.when(lat < lats - 1)
    def _():
        upward().wait_send()
        southward().wait_send()
        downward().wait_recv()

    @pl.when(lat > 0)
    def _():
        downward().wait_send()
        upward().wait_recv()
        southward().wait_recv()

    eastward.wait()
    westward.wait()
    for h, p, g in helper_of:

        @pl.when(lat == h)
        def _():
            for k in order:
                relay(k, counts[1 + g]).wait_send()
                home(g, k, p).wait_send()
            home(g, 0, p).wait_send()

    quiet = jnp.logical_not(is_polar)
    if is_helper is not None:
        quiet = quiet & jnp.logical_not(is_helper)

    @pl.when(quiet)
    def _():
        for copy in bring:
            copy.wait()


def merged_kernel(plans, send_ref, x_hbm, *refs):
    force_plan, plan, parts = plans
    outs = refs[6 : 6 + 6]
    scratch = refs[6 + 6 :]
    x_ref = scratch[0]

    def force():
        force_kernel(force_plan, send_ref, x_hbm, x_ref, *scratch[1:parts])

    circle_kernel(plan, force, x_ref, *refs[0:6], *outs, *scratch[parts:])


def force_and_filter(plan, halves, send, x, wind_east, wind_north, polar_mask, table, high, low):
    _, lons, _, _, _, counts, tracers, levels = plan
    fields, rows, lon_dev = x.shape
    devices, _, width = send.shape
    quarter = high.shape[0]
    steps = levels // level_step(levels)
    lane0 = (lon_dev - 1) // 128 * 128
    depth = 2 * counts[0] * rows
    held = max(counts[1:]) if len(counts) > 1 else 1
    vmem = pl.BlockSpec(memory_space=pltpu.VMEM)
    hbm = pl.BlockSpec(memory_space=pl.ANY)
    f32 = jnp.float32
    groups = max(1, len(counts) - 1)
    column = (steps, rows, 128)
    group = max(1, 512 // (halves * width)) if width == 128 else 1
    span = group * halves * width
    wide = lon_dev + -lon_dev % LANE_STEP
    left = pltpu.VMEM((2 * fields * rows, span), jnp.bfloat16)
    right = pltpu.VMEM((wide, span), jnp.bfloat16)
    dma = pltpu.SemaphoreType.DMA
    force_scratch = [
        pltpu.VMEM(x.shape, f32),
        pltpu.VMEM(send.shape, f32),
        pltpu.VMEM((fields * rows, wide), f32),
        pltpu.VMEM((fields * rows, 128), f32),
        left, left, right, right,
        dma((2,)), dma((devices,)), dma((devices,)),
    ]
    circle_scratch = [
        pltpu.VMEM((lons, counts[0], rows, lon_dev), f32),
        pltpu.VMEM((lons, held, rows, lon_dev), f32),
        pltpu.VMEM(table.shape[1:], f32),
        pltpu.VMEM(high.shape, jnp.bfloat16),
        pltpu.VMEM(low.shape, jnp.bfloat16),
        pltpu.VMEM((4, depth, quarter), jnp.bfloat16),
        pltpu.VMEM((depth, table.shape[2]), jnp.bfloat16),
        pltpu.VMEM((fields, lon_dev), f32),
        pltpu.VMEM((levels, lon_dev), f32),
        pltpu.VMEM((fields, lon_dev), f32),
        pltpu.VMEM(column, f32),
        pltpu.VMEM(column, f32),
        pltpu.VMEM((levels, 8, lon_dev), f32),
        pltpu.VMEM((levels, rows, lon_dev - lane0), f32),
        dma((7,)), dma((lons,)), dma((lons,)), dma((groups * lons,)), dma((lons,)), dma((lons,)),
        dma((lons,)), dma((lons,)), dma((lons,)), dma((lons,)), dma((groups * lons,)),
        dma((5,)), dma((5,)),
    ]
    plans = ((lons, halves, levels, tracers, group), plan, len(force_scratch))
    return pl.pallas_call(
        functools.partial(merged_kernel, plans),
        out_shape=[
            jax.ShapeDtypeStruct(x.shape, f32),
            jax.ShapeDtypeStruct((fields, lon_dev), f32),
            jax.ShapeDtypeStruct((levels, lon_dev), f32),
            jax.ShapeDtypeStruct((fields, lon_dev), f32),
            jax.ShapeDtypeStruct(column, f32),
            jax.ShapeDtypeStruct(column, f32),
        ],
        in_specs=[
            vmem, hbm, hbm, hbm, pl.BlockSpec(memory_space=pltpu.SMEM), hbm, hbm, hbm,
        ],
        out_specs=[vmem] * 6,
        scratch_shapes=force_scratch + circle_scratch,
        compiler_params=pltpu.CompilerParams(
            collective_id=1, has_side_effects=True, vmem_limit_bytes=58 * 1024 * 1024
        ),
    )(send, x, wind_east, wind_north, polar_mask, table, high, low)


def owner_positions(owner_dev, devices):
    count = owner_dev.shape[0]
    span = 128
    one_hot = (owner_dev[:, None] == lax.broadcasted_iota(jnp.int32, (1, devices), 1)).astype(
        jnp.bfloat16
    ).reshape(count // span, span, devices)
    lower = jnp.asarray(np.tril(np.ones((span, span))), jnp.bfloat16)
    inner = jnp.einsum("ij,bjd->bid", lower, one_hot, preferred_element_type=jnp.float32)
    sums = inner[:, -1, :]
    blocks = count // span
    before = jnp.asarray(np.tril(np.ones((blocks, blocks)), -1), jnp.float32)
    offset = jnp.dot(before, sums, precision=lax.Precision.HIGHEST)
    ranks = (inner + offset[:, None, :]) * one_hot.astype(jnp.float32)
    return jnp.sum(ranks, axis=2).reshape(count).astype(jnp.int32) - 1


def shards(
    adjoint_in, wind_east, wind_north, polar_mask, obs_owner, obs_cell, obs_kernel, obs_resid
):
    tracers, levels, lat_dev, lon_dev = adjoint_in.shape
    fields = tracers * levels
    lat_count = lax.axis_size("lat")
    lon_count = lax.axis_size("lon")
    lat_index = lax.axis_index("lat")
    lon_width = lon_dev * lon_count
    total_rows = lat_dev * lat_count
    devices = lat_count * lon_count
    obs_count = obs_owner.shape[0]
    capacity = 2 * obs_count // devices

    owner_dev = obs_owner[:, 0]
    slot_index = owner_dev * capacity + owner_positions(owner_dev, devices)
    payload = jnp.concatenate(
        [
            obs_kernel,
            obs_resid,
            obs_cell.astype(jnp.float32)[:, None],
            jnp.zeros((obs_count, 32 - levels - tracers - 1), jnp.float32),
        ],
        axis=1,
    )
    halves, _, _ = pack_layout(capacity, levels, tracers)
    send = pack_soundings(slot_index, payload, devices, capacity, levels, tracers)
    high, low, waves, weights = circle_tables(lon_width)
    caps = -(-(total_rows // 8) // lat_dev)
    polar = sorted(set(range(caps)) | set(range(lat_count - caps, lat_count)))
    helpers = helper_bands(lat_count)
    share = fields // lon_count
    counts = (share // 2, share // 4, share // 4) if helpers else (share,)
    table = damping_table(polar, lat_dev, total_rows, lon_width, waves, weights)
    plan = (lat_count, lon_count, polar, helpers, share, counts, tracers, levels)
    field, lower, south, upper, right, left = force_and_filter(
        plan, halves, send, adjoint_in.reshape(fields, lat_dev, lon_dev), wind_east, wind_north,
        polar_mask, jnp.asarray(table), jnp.asarray(high), jnp.asarray(low),
    )
    field = field.reshape(tracers, levels, lat_dev, lon_dev)
    keep = (lat_index < lat_count - 1).astype(jnp.int32).reshape(1)
    return advect(keep, field, wind_east, wind_north, lower, south, upper, right, left)


def solution(mesh):
    placed = (
        P(None, None, "lat", "lon"),
        P(None, "lat", "lon"),
        P(None, "lat", "lon"),
        P(),
        P(("lat", "lon"), None),
        P(("lat", "lon")),
        P(("lat", "lon"), None),
        P(("lat", "lon"), None),
    )

    return jax.shard_map(
        shards, mesh=mesh, in_specs=placed, out_specs=P(None, None, "lat", "lon"), check_vma=False
    )
```

```python
import functools
import math

import jax
import jax.numpy as jnp
import ml_dtypes
import numpy as np
from jax import lax
from jax.experimental import pallas as pl
from jax.experimental.pallas import tpu as pltpu
from jax.sharding import PartitionSpec as P

MESH = pl.DeviceIdType.MESH
LANE_STEP = 256
WINDOW = 4


def circle_tables(lon_width):
    width = lon_width // 4
    half = width // 2

    def table(waves, turns, repeats):
        places = np.concatenate([np.arange(width) + width * turn for turn in range(repeats)])
        phase = 2.0 * np.pi * ((places[:, None] * waves[None, :]) % lon_width) / lon_width
        return np.cos(phase - 0.5 * np.pi * turns[None, :])

    zero = np.concatenate([4 * np.arange(half + 1), 4 * np.arange(1, half)])
    zero_turns = np.concatenate([np.zeros(half + 1), np.ones(half - 1)])
    zero_weights = np.where((zero == 0) | (zero == lon_width // 2), 1.0, 2.0)
    two = np.tile(4 * np.arange(half) + 2, 2)
    one = np.tile(4 * np.arange(width) + 1, 2)
    parts = [
        (table(zero, zero_turns, 1), zero, zero_weights / lon_width),
        (table(two, np.repeat([0, 1], half), 1), two, np.full(width, 2.0 / lon_width)),
        (table(one, np.repeat([0, 1], width), 2), one, np.full(2 * width, 2.0 / lon_width)),
    ]
    bases, waves, weights = [], [], []
    for basis, wave, weight in parts:
        extra = -wave.shape[0] % LANE_STEP
        basis = np.pad(basis, ((0, 0), (0, extra)))
        bases += [basis[i : i + width] for i in range(0, basis.shape[0], width)]
        waves.append(np.pad(wave, (0, extra)))
        weights.append(np.pad(weight, (0, extra)))
    basis = np.concatenate(bases, axis=1).astype(np.float32)
    high = basis.astype(ml_dtypes.bfloat16)
    low = (basis - high.astype(np.float32)).astype(ml_dtypes.bfloat16)
    return high, low, np.concatenate(waves), np.concatenate(weights)


def helper_bands(lat_count):
    if lat_count != 8:
        return {}
    return {0: (2, 4), lat_count - 1: (lat_count - 3, lat_count - 5)}


def damping_table(bands, lat_dev, total_rows, lon_width, waves, weights):
    rows = np.asarray(bands)[:, None] * lat_dev + np.arange(lat_dev)[None, :]
    lat_ratio = np.sin(np.pi * (rows + 0.5) / total_rows) / np.sin(
        np.pi * (total_rows // 8) / total_rows
    )
    sine_k = np.sin(np.pi * waves / lon_width)
    damping = lat_ratio[..., None] / np.maximum(sine_k, lat_ratio[..., None])
    return ((damping - 1.0) * weights).astype(np.float32)


def pack_layout(capacity, levels, tracers):
    halves = max(1, capacity // 128)
    rows = halves * (levels + tracers + 1)
    return halves, capacity // halves, rows + -rows % 8


def pack_kernel(levels, tracers, slots_ref, payload_ref, out_ref, placed):
    devices, _, width = out_ref.shape
    halves = placed.shape[0] // (devices * width)
    words = payload_ref.shape[1]
    chunk = 64

    def clear(i, carry):
        where = pl.ds(pl.multiple_of(i * chunk, chunk), chunk)
        placed[where, :] = jnp.zeros((chunk, placed.shape[1]), jnp.float32)
        return carry

    lax.fori_loop(0, placed.shape[0] // chunk, clear, 0)

    def put(i, carry):
        base = pl.multiple_of(i * 16, 16)
        block = payload_ref[pl.ds(base, 16), :]
        slots = [slots_ref[base + j] for j in range(16)]
        for j, slot in enumerate(slots):
            placed[pl.ds(slot, 1), 0:words] = block[j : j + 1, :]
        return carry

    lax.fori_loop(0, payload_ref.shape[0] // 16, put, 0)

    def turn(device, carry):
        for half in range(halves):
            base = pl.multiple_of((device * halves + half) * width, width)
            block = placed[pl.ds(base, width), :].T
            out_ref[device, half * levels : (half + 1) * levels, :] = block[0:levels]
            first = halves * levels + half * tracers
            out_ref[device, first : first + tracers, :] = block[levels : levels + tracers]
            first = halves * (levels + tracers) + half
            out_ref[device, first : first + 1, :] = block[levels + tracers : levels + tracers + 1]
        return carry

    lax.fori_loop(0, devices, turn, 0)


def pack_soundings(slots, payload, devices, capacity, levels, tracers):
    _, width, rows = pack_layout(capacity, levels, tracers)
    return pl.pallas_call(
        functools.partial(pack_kernel, levels, tracers),
        out_shape=jax.ShapeDtypeStruct((devices, rows, width), jnp.float32),
        in_specs=[
            pl.BlockSpec(memory_space=pltpu.SMEM),
            pl.BlockSpec(memory_space=pltpu.VMEM),
        ],
        out_specs=pl.BlockSpec(memory_space=pltpu.VMEM),
        scratch_shapes=[pltpu.VMEM((devices * capacity, 128), jnp.float32)],
        compiler_params=pltpu.CompilerParams(vmem_limit_bytes=32 * 1024 * 1024),
    )(slots, payload)


def force_kernel(
    plan, send_ref, x_hbm, out_ref, recv, total, turned, left0, left1, right0, right1, local_sem, send_sem, recv_sem
):
    lons, halves, levels, tracers, group = plan
    devices, _, width = send_ref.shape
    fields, rows, lon_dev = out_ref.shape
    me = lax.axis_index("lat") * lons + lax.axis_index("lon")
    start = pltpu.make_async_copy(x_hbm, out_ref, local_sem.at[0])
    start.start()
    own = pltpu.make_async_copy(send_ref.at[me], recv.at[me], local_sem.at[1])
    own.start()

    def ahead(k):
        return lax.rem(me + k, devices)

    def behind(k):
        return lax.rem(me + devices - k, devices)

    barrier = pltpu.get_barrier_semaphore()

    def greet(k, carry):
        other = ahead(k)
        pl.semaphore_signal(
            barrier, inc=1, device_id=(other // lons, lax.rem(other, lons)), device_id_type=MESH
        )
        return carry

    lax.fori_loop(1, devices, greet, 0)
    pl.semaphore_wait(barrier, devices - 1)

    def parcel(target, slot):
        return pltpu.make_async_remote_copy(
            src_ref=send_ref.at[target], dst_ref=recv.at[slot],
            send_sem=send_sem.at[target], recv_sem=recv_sem.at[slot],
            device_id=(target // lons, lax.rem(target, lons)), device_id_type=MESH,
        )

    steps = devices // group

    def each(step, act):
        for spot in reversed(range(group)):
            k = step * group + spot
            if spot == 0:

                @pl.when(k > 0)
                def _():
                    act(k)
            else:
                act(k)

    def post(step):
        each(step, lambda k: parcel(ahead(k), me).start())

    for step in range(min(WINDOW, steps)):
        post(step)

    columns = lax.broadcasted_iota(jnp.int32, (right0.shape[0], width), 0).astype(jnp.float32)
    depth = fields * rows

    def build(source, spot, left, right):
        for half in range(halves):
            lanes = slice((spot * halves + half) * width, (spot * halves + half + 1) * width)
            kernel = recv[source, half * levels : (half + 1) * levels, :]
            first = halves * (levels + tracers) + half
            cell = recv[source, first : first + 1, :]
            row = jnp.floor((cell + 0.5) * (1.0 / lon_dev))
            column = cell - row * lon_dev
            contrib = [
                kernel * recv[source, halves * levels + half * tracers + tracer, :][None, :]
                for tracer in range(tracers)
            ]
            contrib = jnp.concatenate(contrib, axis=0)
            top = contrib.astype(jnp.bfloat16)
            rest = (contrib - top.astype(jnp.float32)).astype(jnp.bfloat16)
            for place in range(rows):
                here = jnp.where(row == place, 1.0, 0.0)
                mask = jnp.broadcast_to(here, (16, width)).astype(jnp.bfloat16)
                mask = jnp.concatenate([mask] * (fields // 16), axis=0)
                f = place * fields
                left[f : f + fields, lanes] = top * mask
                left[depth + f : depth + f + fields, lanes] = rest * mask
            right[:, lanes] = jnp.where(columns == column, 1.0, 0.0).astype(jnp.bfloat16)

    def fetch(step):
        each(step, lambda k: parcel(behind(k), behind(k)).wait_recv())
        each(step, lambda k: parcel(ahead(k), me).wait_send())

        @pl.when(step + WINDOW < steps)
        def _():
            post(step + WINDOW)

    def multiply(left, right, first):
        columns = slice(first, first + LANE_STEP)
        product = lax.dot_general(
            left[...], right[columns, :], (((1,), (1,)), ((), ())),
            preferred_element_type=jnp.float32,
        )
        total[:, columns] += product[:depth] + product[depth:]

    def both(step, left, right, old_left, old_right):
        bands = list(range(0, old_right.shape[0], LANE_STEP))
        for spot in range(max(group, len(bands))):
            if spot < group:
                build(behind(step * group + spot), spot, left, right)
            if spot < len(bands):
                multiply(old_left, old_right, bands[spot])

    own.wait()
    total[...] = jnp.zeros_like(total)
    fetch(0)
    for spot in range(group):
        build(behind(spot), spot, left0, right0)

    def pair(i, carry):
        fetch(2 * i + 1)
        both(2 * i + 1, left1, right1, left0, right0)
        fetch(2 * i + 2)
        both(2 * i + 2, left0, right0, left1, right1)
        return carry

    lax.fori_loop(0, steps // 2 - 1, pair, 0)
    fetch(steps - 1)
    both(steps - 1, left1, right1, left0, right0)
    for first in range(0, right1.shape[0], LANE_STEP):
        multiply(left1, right1, first)
    start.wait()
    for first in range(0, lon_dev, 128):
        span = min(128, lon_dev - first)
        for place in range(rows):
            for f in range(0, fields, 8):
                turned[pl.ds(f * rows + place, 8, stride=rows), :] = total[
                    place * fields + f : place * fields + f + 8, first : first + 128
                ]
        out_ref[:, :, first : first + span] += turned[:, 0:span].reshape(fields, rows, span)


def level_step(levels):
    return 8 if levels % 8 == 0 else 1


def stencil_kernel(
    keep_ref, field_ref, east_ref, north_ref, lower_ref, south_ref, upper_ref, right_ref, left_ref, out_ref,
    wide, edge,
):
    tracers, step, rows, width = field_ref.shape
    levels = upper_ref.shape[0] // tracers
    padded = wide.shape[1]
    lanes = lax.broadcasted_iota(jnp.int32, (rows, padded), 1)
    subs = lax.broadcasted_iota(jnp.int32, (rows, padded), 0)
    keep = keep_ref[0]
    first = pl.program_id(0) * step
    right = right_ref[0]
    left = left_ref[0]

    def widened(slot, block):
        wide[slot * rows : (slot + 1) * rows, 0:width] = block
        return wide[slot * rows : (slot + 1) * rows, :]

    for level in range(step):
        for tracer in range(tracers):
            place = tracer * levels + first + level
            edge[tracer : tracer + 1, 0:width] = upper_ref[pl.ds(place, 1), :]
            edge[tracers + tracer : tracers + tracer + 1, 0:width] = lower_ref[pl.ds(place, 1), :]
        edge[2 * tracers : 2 * tracers + 1, 0:width] = south_ref[pl.ds(first + level, 1), :]
        lane = tracers * step + level
        wind_east = widened(0, east_ref[level])
        wind_west = jnp.where(
            lanes == 0, left[:, lane : lane + 1], pltpu.roll(wind_east, 1, 1)
        )
        wind_north = widened(1, north_ref[level])
        wind_south = jnp.where(
            subs == 0, edge[2 * tracers : 2 * tracers + 1, :], pltpu.roll(wind_north, 1, 0)
        )
        wind_north = jnp.where((subs == rows - 1) & (keep == 0), 0.0, wind_north)
        east_face = jnp.maximum(wind_east, 0.0)
        west_face = jnp.minimum(wind_west, 0.0)
        north_face = jnp.maximum(wind_north, 0.0)
        south_face = jnp.minimum(wind_south, 0.0)
        for tracer in range(tracers):
            other = tracers + tracer
            lane = tracer * step + level
            center = widened(2 + tracer, field_ref[tracer, level])
            east_val = jnp.where(
                lanes == width - 1, right[:, lane : lane + 1], pltpu.roll(center, padded - 1, 1)
            )
            west_val = jnp.where(lanes == 0, left[:, lane : lane + 1], pltpu.roll(center, 1, 1))
            upper_val = jnp.where(
                subs == rows - 1, edge[tracer : tracer + 1, :], pltpu.roll(center, rows - 1, 0)
            )
            lower_val = jnp.where(subs == 0, edge[other : other + 1, :], pltpu.roll(center, 1, 0))
            result = center + east_face * (east_val - center) + west_face * (center - west_val)
            result = result + north_face * (upper_val - center) + south_face * (center - lower_val)
            out_ref[tracer, level] = result[:, 0:width]


def advect(keep, field, wind_east, wind_north, lower, south, upper, right, left):
    tracers, levels, rows, width = field.shape
    step = level_step(levels)
    padded = -(-(width + 1) // 128) * 128

    def four(depth, span):
        return pl.BlockSpec((tracers, step, depth, span), lambda i: (0, i, 0, 0))

    def three(depth, span):
        return pl.BlockSpec((step, depth, span), lambda i: (i, 0, 0))

    def whole(array):
        return pl.BlockSpec(array.shape, lambda i: (0, 0))

    column = pl.BlockSpec((1, rows, 128), lambda i: (i, 0, 0))
    return pl.pallas_call(
        stencil_kernel,
        grid=(levels // step,),
        out_shape=jax.ShapeDtypeStruct(field.shape, jnp.float32),
        in_specs=[
            pl.BlockSpec(memory_space=pltpu.SMEM),
            four(rows, width), three(rows, width), three(rows, width),
            whole(lower), whole(south), whole(upper), column, column,
        ],
        out_specs=four(rows, width),
        scratch_shapes=[
            pltpu.VMEM(((2 + tracers) * rows, padded), jnp.float32),
            pltpu.VMEM((8, padded), jnp.float32),
        ],
        compiler_params=pltpu.CompilerParams(vmem_limit_bytes=60 * 1024 * 1024),
    )(keep, field, wind_east, wind_north, lower, south, upper, right, left)


def circle_kernel(
    plan, force, x_ref, we_ref, wn_ref, mask_ref, table_hbm, high_hbm, low_hbm,
    filt_ref, lower_ref, south_ref, upper_ref, right_ref, left_ref,
    recv, hold, fac_ref, high, low, pieces, spectra, low_out, south_out, up_out, right_out, left_out,
    wind_rows, wind_cols, local_sem, direct_send, direct_recv, out_send, out_recv, relay_send, relay_recv,
    back_send, back_recv, home_send, home_recv, edge_send, edge_recv,
):
    lats, lons, polar, helpers, share, counts, tracers, levels = plan
    fields, rows, lon_dev = x_ref.shape
    quarter = high.shape[0]
    blocks = quarter // lon_dev
    lat = lax.axis_index("lat")
    z = lax.axis_index("lon")
    groups = len(counts) - 1
    helper_of = [(h, p, g) for p in helpers for g, h in enumerate(helpers[p])]

    def among(choices):
        found = lat == choices[0]
        for choice in choices[1:]:
            found = found | (lat == choice)
        return found

    is_polar = among(polar)
    is_helper = among([h for h, _, _ in helper_of]) if helper_of else None

    def ahead(k):
        return lax.rem(z + k, lons)

    def behind(k):
        return lax.rem(z + lons - k, lons)

    bring = [
        pltpu.make_async_copy(high_hbm, high, local_sem.at[0]),
        pltpu.make_async_copy(low_hbm, low, local_sem.at[1]),
    ]
    for copy in bring:
        copy.start()
    lane0 = (lon_dev - 1) // 128 * 128
    winds = [
        pltpu.make_async_copy(wn_ref.at[:, pl.ds(rows - 8, 8), :], wind_rows, local_sem.at[2]),
        pltpu.make_async_copy(
            we_ref.at[:, :, pl.ds(lane0, lon_dev - lane0)], wind_cols, local_sem.at[3]
        ),
    ]
    for copy in winds:
        copy.start()

    force()

    offsets = [sum(counts[:i]) for i in range(len(counts))]
    order = sorted(range(1, lons), key=lambda k: -min(k, lons - k))

    def remote(src, dst, send, took, where):
        return pltpu.make_async_remote_copy(
            src_ref=src, dst_ref=dst, send_sem=send, recv_sem=took,
            device_id=where, device_id_type=MESH,
        )

    def direct(k):
        return remote(
            x_ref.at[pl.ds(share * ahead(k), counts[0])], recv.at[z, pl.ds(0, counts[0])],
            direct_send.at[k], direct_recv.at[k], (lat, ahead(k)),
        )

    def outward(g, k, where):
        count = counts[1 + g]
        slot = recv.at[z, pl.ds(0, count)] if k == 0 else hold.at[ahead(k)]
        return remote(
            x_ref.at[pl.ds(share * ahead(k) + offsets[1 + g], count)], slot,
            out_send.at[g * lons + k], out_recv.at[k], (where, z),
        )

    def relay(k, count):
        return remote(
            hold.at[ahead(k)], recv.at[z, pl.ds(0, count)],
            relay_send.at[k], relay_recv.at[k], (lat, ahead(k)),
        )

    def back(k):
        return remote(
            recv.at[ahead(k), pl.ds(0, counts[0])], filt_ref.at[pl.ds(share * z, counts[0])],
            back_send.at[k], back_recv.at[k], (lat, ahead(k)),
        )

    def home(g, k, where):
        count = counts[1 + g]
        return remote(
            recv.at[ahead(k), pl.ds(0, count)],
            filt_ref.at[pl.ds(share * z + offsets[1 + g], count)],
            home_send.at[k], home_recv.at[g * lons + k], (where, ahead(k)),
        )

    def factors(band):
        return pltpu.make_async_copy(
            table_hbm.at[polar.index(band)], fac_ref, local_sem.at[6]
        )

    def filter_share(count, band):
        depth = count * rows
        factors(band).wait()
        subs = lax.broadcasted_iota(jnp.int32, (rows, 1), 0)
        live = jnp.zeros((rows, 1), jnp.float32)
        for row in range(rows):
            filtered = mask_ref[band * rows + row].astype(jnp.float32)
            live = jnp.where(subs == row, filtered, live)
        fac_ref[...] = fac_ref[...] * live

        def quarter_of(i, f):
            held = [recv[i * blocks + j, f] for j in range(blocks)]
            return held[0] if blocks == 1 else jnp.concatenate(held, axis=1)

        for f in range(count):
            q = [quarter_of(i, f) for i in range(4)]
            even, odd = q[0] + q[2], q[1] + q[3]
            for p, part in enumerate((even + odd, even - odd, q[0] - q[2], q[1] - q[3])):
                top = part.astype(jnp.bfloat16)
                rest = (part - top.astype(jnp.float32)).astype(jnp.bfloat16)
                pieces[p, f * rows : (f + 1) * rows, :] = top
                pieces[p, depth + f * rows : depth + (f + 1) * rows, :] = rest

        single = high.shape[1] // 6
        spans = [(0, single), (single, 2 * single), (2 * single, 4 * single), (4 * single, 6 * single)]

        def forward(p):
            begin, end = spans[p]
            both = jnp.dot(
                pieces[p, 0 : 2 * depth, :], high[:, begin:end], preferred_element_type=jnp.float32
            )
            small = jnp.dot(
                pieces[p, 0:depth, :], low[:, begin:end], preferred_element_type=jnp.float32
            )
            return both[:depth] + both[depth:] + small

        def damped(values, begin):
            end = begin + values.shape[1]
            values = values.reshape(count, rows, end - begin) * fac_ref[:, begin:end][None]
            values = values.reshape(depth, end - begin)
            top = values.astype(jnp.bfloat16)
            spectra[0:depth, begin:end] = top
            spectra[depth : 2 * depth, begin:end] = (values - top.astype(jnp.float32)).astype(
                jnp.bfloat16
            )

        damped(forward(0), 0)
        damped(forward(1), single)
        damped(forward(2) + forward(3), 2 * single)

        def inverse(p):
            begin, end = spans[p]
            first = min(begin, 2 * single)
            last = first + end - begin
            sides = (((1,), (1,)), ((), ()))
            both = lax.dot_general(
                spectra[0 : 2 * depth, first:last], high[:, begin:end], sides,
                preferred_element_type=jnp.float32,
            )
            small = lax.dot_general(
                spectra[0:depth, first:last], low[:, begin:end], sides,
                preferred_element_type=jnp.float32,
            )
            return both[:depth] + both[depth:] + small

        zero_part, two_part = inverse(0), inverse(1)
        first, second = inverse(2), inverse(3)
        even_part, odd_part = zero_part + two_part, zero_part - two_part
        results = [even_part + first, odd_part + second, even_part - first, odd_part - second]
        for i in range(4):
            for j in range(blocks):
                change = results[i][:, j * lon_dev : (j + 1) * lon_dev]
                change = change.reshape(count, rows, lon_dev)
                place = i * blocks + j
                recv[place, 0:count] = recv[place, 0:count] + change

    def southward():
        return remote(south_out, south_ref, edge_send.at[4], edge_recv.at[4], (lat + 1, z))

    for copy in winds:
        copy.wait()
    south_out[...] = wind_rows[:, 7, :]

    @pl.when(lat < lats - 1)
    def _():
        southward().start()

    for band in polar:
        friends = helpers.get(band, ())

        @pl.when(lat == band)
        def _():
            n0 = counts[0] if friends else share
            factors(band).start()
            for k in order:
                direct(k).start()
            for k in order + [0]:
                for g, h in enumerate(friends):
                    outward(g, k, h).start()
                for g, h in enumerate(friends):
                    outward(g, k, h).wait_send()
            own = pltpu.make_async_copy(
                x_ref.at[pl.ds(share * z, n0)], recv.at[z, pl.ds(0, n0)], local_sem.at[4]
            )
            own.start()
            own.wait()
            for k in order:
                direct(k).wait_recv()
            for copy in bring:
                copy.wait()
            filter_share(n0, band)
            for k in order:
                back(k).start()
            mine = pltpu.make_async_copy(
                recv.at[z, pl.ds(0, n0)], filt_ref.at[pl.ds(share * z, n0)], local_sem.at[5]
            )
            mine.start()
            mine.wait()
            for k in order:
                direct(k).wait_send()
                back(k).wait_send()
                back(k).wait_recv()
            for g, h in enumerate(friends):
                for k in range(lons):
                    home(g, k, h).wait_recv()

    for h, p, g in helper_of:

        @pl.when(lat == h)
        def _():
            factors(p).start()
            for k in order:
                outward(g, k, p).wait_recv()
                relay(k, counts[1 + g]).start()
            outward(g, 0, p).wait_recv()
            for k in order:
                relay(k, counts[1 + g]).wait_recv()
            for copy in bring:
                copy.wait()
            filter_share(counts[1 + g], p)
            for k in order:
                home(g, k, p).start()
            home(g, 0, p).start()

    @pl.when(jnp.logical_not(is_polar))
    def _():
        filt_ref[...] = x_ref[...]

    low_out[...] = filt_ref[:, rows - 1, :]
    up_out[...] = filt_ref[:, 0, :]

    def upward():
        return remote(low_out, lower_ref, edge_send.at[0], edge_recv.at[0], (lat + 1, z))

    def downward():
        return remote(up_out, upper_ref, edge_send.at[1], edge_recv.at[1], (lat - 1, z))

    @pl.when(lat < lats - 1)
    def _():
        upward().start()

    @pl.when(lat > 0)
    def _():
        downward().start()

    step = level_step(levels)
    lanes = lax.broadcasted_iota(jnp.int32, (rows, 128), 1)
    for i in range(levels // step):
        to_left = jnp.zeros((rows, 128), jnp.float32)
        to_right = jnp.zeros((rows, 128), jnp.float32)
        for level in range(step):
            for tracer in range(tracers):
                f = tracer * levels + i * step + level
                spot = lanes == tracer * step + level
                to_left = jnp.where(spot, filt_ref[f, :, 0:1], to_left)
                to_right = jnp.where(spot, filt_ref[f, :, lon_dev - 1 : lon_dev], to_right)
            column = wind_cols[i * step + level, :, lon_dev - 1 - lane0 : lon_dev - lane0]
            to_right = jnp.where(lanes == tracers * step + level, column, to_right)
        left_out[i] = to_left
        right_out[i] = to_right

    eastward = remote(right_out, left_ref, edge_send.at[2], edge_recv.at[2], (lat, ahead(1)))
    westward = remote(left_out, right_ref, edge_send.at[3], edge_recv.at[3], (lat, behind(1)))
    eastward.start()
    westward.start()

    @pl.when(lat == 0)
    def _():
        lower_ref[...] = jnp.zeros_like(lower_ref)
        south_ref[...] = jnp.zeros_like(south_ref)

    @pl.when(lat == lats - 1)
    def _():
        upper_ref[...] = jnp.zeros_like(upper_ref)

    @pl.when(lat < lats - 1)
    def _():
        upward().wait_send()
        southward().wait_send()
        downward().wait_recv()

    @pl.when(lat > 0)
    def _():
        downward().wait_send()
        upward().wait_recv()
        southward().wait_recv()

    eastward.wait()
    westward.wait()
    for h, p, g in helper_of:

        @pl.when(lat == h)
        def _():
            for k in order:
                relay(k, counts[1 + g]).wait_send()
                home(g, k, p).wait_send()
            home(g, 0, p).wait_send()

    quiet = jnp.logical_not(is_polar)
    if is_helper is not None:
        quiet = quiet & jnp.logical_not(is_helper)

    @pl.when(quiet)
    def _():
        for copy in bring:
            copy.wait()


def merged_kernel(plans, send_ref, x_hbm, *refs):
    force_plan, plan, parts = plans
    outs = refs[6 : 6 + 6]
    scratch = refs[6 + 6 :]
    x_ref = scratch[0]

    def force():
        force_kernel(force_plan, send_ref, x_hbm, x_ref, *scratch[1:parts])

    circle_kernel(plan, force, x_ref, *refs[0:6], *outs, *scratch[parts:])


def force_and_filter(plan, halves, send, x, wind_east, wind_north, polar_mask, table, high, low):
    _, lons, _, _, _, counts, tracers, levels = plan
    fields, rows, lon_dev = x.shape
    devices, _, width = send.shape
    quarter = high.shape[0]
    steps = levels // level_step(levels)
    lane0 = (lon_dev - 1) // 128 * 128
    depth = 2 * counts[0] * rows
    held = max(counts[1:]) if len(counts) > 1 else 1
    vmem = pl.BlockSpec(memory_space=pltpu.VMEM)
    hbm = pl.BlockSpec(memory_space=pl.ANY)
    f32 = jnp.float32
    groups = max(1, len(counts) - 1)
    column = (steps, rows, 128)
    group = max(1, 512 // (halves * width)) if width == 128 else 1
    span = group * halves * width
    wide = lon_dev + -lon_dev % LANE_STEP
    left = pltpu.VMEM((2 * fields * rows, span), jnp.bfloat16)
    right = pltpu.VMEM((wide, span), jnp.bfloat16)
    dma = pltpu.SemaphoreType.DMA
    force_scratch = [
        pltpu.VMEM(x.shape, f32),
        pltpu.VMEM(send.shape, f32),
        pltpu.VMEM((fields * rows, wide), f32),
        pltpu.VMEM((fields * rows, 128), f32),
        left, left, right, right,
        dma((2,)), dma((devices,)), dma((devices,)),
    ]
    circle_scratch = [
        pltpu.VMEM((lons, counts[0], rows, lon_dev), f32),
        pltpu.VMEM((lons, held, rows, lon_dev), f32),
        pltpu.VMEM(table.shape[1:], f32),
        pltpu.VMEM(high.shape, jnp.bfloat16),
        pltpu.VMEM(low.shape, jnp.bfloat16),
        pltpu.VMEM((4, depth, quarter), jnp.bfloat16),
        pltpu.VMEM((depth, table.shape[2]), jnp.bfloat16),
        pltpu.VMEM((fields, lon_dev), f32),
        pltpu.VMEM((levels, lon_dev), f32),
        pltpu.VMEM((fields, lon_dev), f32),
        pltpu.VMEM(column, f32),
        pltpu.VMEM(column, f32),
        pltpu.VMEM((levels, 8, lon_dev), f32),
        pltpu.VMEM((levels, rows, lon_dev - lane0), f32),
        dma((7,)), dma((lons,)), dma((lons,)), dma((groups * lons,)), dma((lons,)), dma((lons,)),
        dma((lons,)), dma((lons,)), dma((lons,)), dma((lons,)), dma((groups * lons,)),
        dma((5,)), dma((5,)),
    ]
    plans = ((lons, halves, levels, tracers, group), plan, len(force_scratch))
    return pl.pallas_call(
        functools.partial(merged_kernel, plans),
        out_shape=[
            jax.ShapeDtypeStruct(x.shape, f32),
            jax.ShapeDtypeStruct((fields, lon_dev), f32),
            jax.ShapeDtypeStruct((levels, lon_dev), f32),
            jax.ShapeDtypeStruct((fields, lon_dev), f32),
            jax.ShapeDtypeStruct(column, f32),
            jax.ShapeDtypeStruct(column, f32),
        ],
        in_specs=[
            vmem, hbm, hbm, hbm, pl.BlockSpec(memory_space=pltpu.SMEM), hbm, hbm, hbm,
        ],
        out_specs=[vmem] * 6,
        scratch_shapes=force_scratch + circle_scratch,
        compiler_params=pltpu.CompilerParams(
            collective_id=1, has_side_effects=True, vmem_limit_bytes=58 * 1024 * 1024
        ),
    )(send, x, wind_east, wind_north, polar_mask, table, high, low)


def owner_positions(owner_dev, devices):
    count = owner_dev.shape[0]
    span = 128
    one_hot = (owner_dev[:, None] == lax.broadcasted_iota(jnp.int32, (1, devices), 1)).astype(
        jnp.bfloat16
    ).reshape(count // span, span, devices)
    lower = jnp.asarray(np.tril(np.ones((span, span))), jnp.bfloat16)
    inner = jnp.einsum("ij,bjd->bid", lower, one_hot, preferred_element_type=jnp.float32)
    sums = inner[:, -1, :]
    blocks = count // span
    before = jnp.asarray(np.tril(np.ones((blocks, blocks)), -1), jnp.float32)
    offset = jnp.dot(before, sums, precision=lax.Precision.HIGHEST)
    ranks = (inner + offset[:, None, :]) * one_hot.astype(jnp.float32)
    return jnp.sum(ranks, axis=2).reshape(count).astype(jnp.int32) - 1


def shards(
    adjoint_in, wind_east, wind_north, polar_mask, obs_owner, obs_cell, obs_kernel, obs_resid
):
    tracers, levels, lat_dev, lon_dev = adjoint_in.shape
    fields = tracers * levels
    lat_count = lax.axis_size("lat")
    lon_count = lax.axis_size("lon")
    lat_index = lax.axis_index("lat")
    lon_width = lon_dev * lon_count
    total_rows = lat_dev * lat_count
    devices = lat_count * lon_count
    obs_count = obs_owner.shape[0]
    capacity = 2 * obs_count // devices

    owner_dev = obs_owner[:, 0]
    slot_index = owner_dev * capacity + owner_positions(owner_dev, devices)
    payload = jnp.concatenate(
        [
            obs_kernel,
            obs_resid,
            obs_cell.astype(jnp.float32)[:, None],
            jnp.zeros((obs_count, 32 - levels - tracers - 1), jnp.float32),
        ],
        axis=1,
    )
    halves, _, _ = pack_layout(capacity, levels, tracers)
    send = pack_soundings(slot_index, payload, devices, capacity, levels, tracers)
    high, low, waves, weights = circle_tables(lon_width)
    caps = -(-(total_rows // 8) // lat_dev)
    polar = sorted(set(range(caps)) | set(range(lat_count - caps, lat_count)))
    helpers = helper_bands(lat_count)
    share = fields // lon_count
    counts = (share // 2, share // 4, share // 4) if helpers else (share,)
    table = damping_table(polar, lat_dev, total_rows, lon_width, waves, weights)
    plan = (lat_count, lon_count, polar, helpers, share, counts, tracers, levels)
    field, lower, south, upper, right, left = force_and_filter(
        plan, halves, send, adjoint_in.reshape(fields, lat_dev, lon_dev), wind_east, wind_north,
        polar_mask, jnp.asarray(table), jnp.asarray(high), jnp.asarray(low),
    )
    field = field.reshape(tracers, levels, lat_dev, lon_dev)
    keep = (lat_index < lat_count - 1).astype(jnp.int32).reshape(1)
    return advect(keep, field, wind_east, wind_north, lower, south, upper, right, left)


def solution(mesh):
    placed = (
        P(None, None, "lat", "lon"),
        P(None, "lat", "lon"),
        P(None, "lat", "lon"),
        P(),
        P(("lat", "lon"), None),
        P(("lat", "lon")),
        P(("lat", "lon"), None),
        P(("lat", "lon"), None),
    )

    return jax.shard_map(
        shards, mesh=mesh, in_specs=placed, out_specs=P(None, None, "lat", "lon"), check_vma=False
    )
```
